128 devices in a mesh: wave: 16 (over x, z_hi, core), lev: 8 (over y, z_lo).
Axes of the slice: x: 4, y: 4, z: 4 (z_hi: 2, z_lo: 2; z = z_hi * 2 + z_lo), core: 2. Of those that a mesh axis runs over, the one named last changes fastest.
Arguments:
- spectra: bfloat16 [1280, 1280, 2, 32], P(('wave', 'lev')), may hold values from -0.125 to 0.125
- legendre: bfloat16 [1280, 640, 1280], P(('wave', 'lev')), may hold values from -0.15625 to 0.15625
- gauss_weights: float32 [640], replicated, may hold values from 0.25 to 1.75
- phys_matrix: float32 [32, 32], replicated, may hold values from -1 to 1
- phys_bias: float32 [32], replicated, may hold values from -3 to 3
- tracers: float32 [8, 64, 320, 640], P(None, None, 'wave', 'lev'), may hold values from 0.2 to 5
- reaction: float32 [64, 64], replicated, may hold values from -0.375 to 0.375
- heat_coeff: float32 [64], replicated, may hold values from -0.625 to 0.625
Outputs:
- spectral_tend: bfloat16 [1280, 1280, 2, 32], P(('wave', 'lev'))
- mixing: float32 [8, 64, 320, 640], P(None, None, 'wave', 'lev')
The draws below stay inside these ranges and needn't reach their ends.
All inputs are finite; a program needn't handle non-finite values.
Results may differ from the reference program's by a relative error of at most 0.007.
Values may be sent and summed in bfloat16 or wider, within the bound.
No kernel may reach another device: no remote copies, remote signals or barrier semaphores. Data moves between devices by JAX's collectives and lax.ppermute only.
A program may use at most 192 MiB of HBM per device.

```python
import math
import jax
import jax.numpy as jnp
from jax import lax

TRUNC = 1280
NLAT = 1280
NLON = 2560
LEV = 8
NT = 64
SUBSTEPS = 2
FL = 32
CLAT = 320
CLON = 640


def block_scale(key, extent, split, least, top_value):
    def one(axis_at, blocks):
        steps = jax.random.uniform(jax.random.fold_in(jax.random.fold_in(key, 6), axis_at), (blocks,), jnp.float32, least / len(split), top_value / len(split))
        return jnp.repeat(jnp.exp(steps), extent[axis_at] // blocks).reshape((-1,) + (1,) * (len(extent) - axis_at - 1))

    gain = one(*split[0])
    for cut in split[1:]:
        gain = gain * one(*cut)
    return gain


def centred(stream_key, shape, spread, most, cuts=(), held_as=jnp.bfloat16):
    gain = block_scale(stream_key, shape, cuts, -0.22, 0.18) if cuts else 1.0
    drawn = jax.random.normal(stream_key, shape, jnp.float32) * spread * gain
    return jnp.minimum(jnp.maximum(drawn, -most), most).astype(held_as)


def setup_inputs(seed: int = 0) -> dict:
    arg_keys = jax.random.split(jax.random.key(seed), 9)
    spectra = centred(arg_keys[0], (TRUNC, TRUNC, 2, FL), 0.02, 0.125, ((0, 128),))
    legendre = centred(arg_keys[1], (TRUNC, NLAT // 2, TRUNC), TRUNC ** -0.5, 0.15625, ((0, 128),))
    gauss_weights = jnp.clip(1.0 + 0.15 * jax.random.normal(arg_keys[2], (NLAT // 2,), jnp.float32), 0.25, 1.75)
    phys_matrix = centred(arg_keys[3], (FL, FL), FL ** -0.5, 1.0, (), jnp.float32)
    phys_bias = centred(arg_keys[4], (FL,), 0.5, 3.0, (), jnp.float32)
    tracers = jnp.clip(jnp.exp(math.log(5.0) - 3.218876 * jax.random.uniform(arg_keys[5], (LEV, NT, CLAT, CLON), jnp.float32) ** block_scale(arg_keys[5], (LEV, NT, CLAT, CLON), ((2, 16), (3, 8)), -0.2, 0.2)), 0.2, 5.0)
    reaction = centred(arg_keys[6], (NT, NT), (4 * NT) ** -0.5, 0.375, (), jnp.float32)
    heat_coeff = centred(arg_keys[7], (NT,), 0.1, 0.625, (), jnp.float32)
    return dict(spectra=spectra, legendre=legendre, gauss_weights=gauss_weights, phys_matrix=phys_matrix, phys_bias=phys_bias, tracers=tracers, reaction=reaction, heat_coeff=heat_coeff)


courant = 0.6

def spectral_keep(m_index, k_index):
    valid_rows = k_index[None, :] < (TRUNC - m_index)[:, None]
    imag_ok = jnp.stack([m_index >= 0, m_index > 0], axis=1)
    return valid_rows[:, :, None] & imag_ok[:, None, :]

def fourier_table(m_rows, inverse):
    lon_index = jnp.arange(NLON, dtype=jnp.int32)
    phase_index = m_rows[:, None] * lon_index[None, :] % NLON
    phase_angle = phase_index.astype(jnp.float32) * (2.0 * math.pi / NLON)
    if inverse:
        factor = jnp.where(m_rows == 0, 1.0, 2.0).astype(jnp.float32)[:, None]
    else:
        factor = jnp.ones((m_rows.shape[0], 1), jnp.float32) / math.sqrt(NLON)
    return jnp.stack([factor * jnp.cos(phase_angle), -factor * jnp.sin(phase_angle)], axis=1).astype(jnp.bfloat16)

def coarse_winds(column_data, levels, chem_rows, chem_cols):
    lat_ratio = column_data.shape[0] // chem_rows
    lon_ratio = column_data.shape[2] // chem_cols

    def coarse(field_block):
        shaped = field_block.reshape(chem_rows, lat_ratio, levels, chem_cols, lon_ratio)
        return shaped.mean(axis=(1, 4)).transpose(1, 0, 2)
    return (coarse(column_data[:, :levels]), coarse(column_data[:, levels:2 * levels]))

def advect_react(padded, row_first, total_rows, reaction):
    wind_u = padded[:, 0]
    wind_v = padded[:, 1]
    mixing = padded[:, 2:]
    face_u = 0.5 * (wind_u[:, :, :-1] + wind_u[:, :, 1:])
    east_flux = courant * (jnp.maximum(face_u, 0.0)[:, None] * mixing[..., :-1] + jnp.minimum(face_u, 0.0)[:, None] * mixing[..., 1:])
    face_v = 0.5 * (wind_v[:, :-1, :] + wind_v[:, 1:, :])
    upper_rows = row_first + jnp.arange(face_v.shape[1], dtype=jnp.int32)
    inside = (upper_rows >= 0) & (upper_rows + 1 <= total_rows - 1)
    face_v = jnp.where(inside[None, :, None], face_v, 0.0)
    south_flux = courant * (jnp.maximum(face_v, 0.0)[:, None] * mixing[:, :, :-1, :] + jnp.minimum(face_v, 0.0)[:, None] * mixing[:, :, 1:, :])
    moved_mix = mixing[:, :, 1:-1, 1:-1] - (east_flux[:, :, 1:-1, 1:] - east_flux[:, :, 1:-1, :-1]) - (south_flux[:, :, 1:, 1:-1] - south_flux[:, :, :-1, 1:-1])
    reacted_mix = moved_mix + jnp.einsum('st,ltrc->lsrc', reaction, moved_mix, precision=lax.Precision.HIGHEST)
    return jnp.concatenate([wind_u[:, None, 1:-1, 1:-1], wind_v[:, None, 1:-1, 1:-1], reacted_mix], axis=1)

def add_heat(physics, heating, levels):
    lat_ratio = physics.shape[0] // heating.shape[1]
    lon_ratio = physics.shape[2] // heating.shape[2]
    spread_heat = jnp.repeat(jnp.repeat(heating, lat_ratio, axis=1), lon_ratio, axis=2).transpose(1, 0, 2)
    return jnp.concatenate([physics[:, :2 * levels], physics[:, 2 * levels:3 * levels] + spread_heat, physics[:, 3 * levels:]], axis=1)

def reference(spectra, legendre, gauss_weights, phys_matrix, phys_bias, tracers, reaction, heat_coeff):
    highest = lax.Precision.HIGHEST
    m_index = jnp.arange(TRUNC, dtype=jnp.int32)
    k_index = jnp.arange(TRUNC, dtype=jnp.int32)
    keep_mask = spectral_keep(m_index, k_index)
    parity = jnp.where(k_index % 2 == 0, 1.0, -1.0).astype(jnp.float32)
    pair_width = 2 * FL

    def inverse_one(pieces):
        spectrum, table, keep_one = pieces
        masked = jnp.where(keep_one[..., None], spectrum.astype(jnp.float32), 0.0).reshape(TRUNC, pair_width)
        stacked_rhs = jnp.concatenate([masked, masked * parity[:, None]], axis=1)
        project = jnp.dot(table.astype(jnp.float32), stacked_rhs, precision=highest)
        north_part = project[:, :pair_width]
        south_part = jnp.flip(project[:, pair_width:], axis=0)
        return jnp.concatenate([north_part, south_part], axis=0).astype(jnp.bfloat16).reshape(NLAT, 2, FL)
    fourier = lax.optimization_barrier(lax.map(inverse_one, (spectra, legendre, keep_mask)))
    inverse_table = fourier_table(m_index, True)
    grid_values = jnp.einsum('mlcf,mcj->lfj', fourier.astype(jnp.float32), inverse_table.astype(jnp.float32), precision=highest).astype(jnp.bfloat16)
    column_data = lax.optimization_barrier(grid_values).astype(jnp.float32)
    physics = jnp.tanh(jnp.einsum('ef,lfj->lej', phys_matrix, column_data, precision=highest) + phys_bias[None, :, None])
    wind_u, wind_v = coarse_winds(column_data, LEV, CLAT, CLON)
    chem_state = jnp.concatenate([wind_u[:, None], wind_v[:, None], tracers], axis=1)

    def chem_level(level_state):
        current = level_state[None]
        for substep in range(SUBSTEPS):
            wrapped = jnp.concatenate([current[..., -1:], current, current[..., :1]], axis=3)
            padded = jnp.pad(wrapped, ((0, 0), (0, 0), (1, 1), (0, 0)))
            current = advect_react(padded, -1, CLAT, reaction)
        return current[0]
    chem_state = lax.map(chem_level, chem_state)
    mixing = chem_state[:, 2:]
    heating = jnp.einsum('t,ltrc->lrc', heat_coeff, mixing, precision=highest)
    tendency = add_heat(physics, heating, LEV).astype(jnp.bfloat16)
    tendency = lax.optimization_barrier(tendency)
    direct_table = fourier_table(m_index, False)
    coeffs = jnp.einsum('lfj,mcj->mlcf', tendency.astype(jnp.float32), direct_table.astype(jnp.float32), precision=highest).astype(jnp.bfloat16)
    coeffs = lax.optimization_barrier(coeffs)
    even_rows = (k_index % 2 == 0)[:, None]

    def direct_one(pieces):
        coeff_one, table, keep_one = pieces
        values = coeff_one.astype(jnp.float32).reshape(NLAT, pair_width)
        north_part = values[:NLAT // 2]
        south_part = jnp.flip(values[NLAT // 2:], axis=0)
        weights = gauss_weights[:, None]
        paired = jnp.concatenate([weights * (north_part + south_part), weights * (north_part - south_part)], axis=1)
        paired = lax.optimization_barrier(paired.astype(jnp.bfloat16)).astype(jnp.float32)
        folded = jnp.dot(table.astype(jnp.float32).T, paired, precision=highest)
        chosen = jnp.where(even_rows, folded[:, :pair_width], folded[:, pair_width:]).reshape(TRUNC, 2, FL)
        return jnp.where(keep_one[..., None], chosen, 0.0).astype(jnp.bfloat16)
    spectral_tend = lax.map(direct_one, (coeffs, legendre, keep_mask))
    return (spectral_tend, mixing)
```

```python
import functools
import math

import jax
import jax.numpy as jnp
from jax import lax
from jax.experimental import pallas as pl
from jax.experimental.pallas import tpu as pltpu
from jax.sharding import PartitionSpec as P

TRUNC = 1280
NLON = 2560
SUBSTEPS = 2
COURANT = 0.6
LANES = 128
HALO = 2
BF, F32 = jnp.bfloat16, jnp.float32


def spectral_keep(m_index, k_index):
    valid_rows = k_index[None, :] < (TRUNC - m_index)[:, None]
    imag_ok = jnp.stack([m_index >= 0, m_index > 0], axis=1)
    return valid_rows[:, :, None] & imag_ok[:, None, :]


def angle_parts():
    m = jnp.arange(TRUNC, dtype=jnp.int32)[:, None]
    unit = 2.0 * math.pi / NLON
    coarse = (m * (LANES * jnp.arange(LANES, dtype=jnp.int32))[None, :] % NLON).astype(F32) * unit
    fine = (m * jnp.arange(LANES, dtype=jnp.int32)[None, :] % NLON).astype(F32) * unit
    return jnp.cos(coarse), jnp.sin(coarse), jnp.cos(fine), jnp.sin(fine)


def table_kernel(a_ref, b_ref, cos_ref, sin_ref, out_ref):
    for block in range(NLON // LANES):
        out_ref[:, block * LANES : (block + 1) * LANES] = (
            a_ref[:, block : block + 1] * cos_ref[...] - b_ref[:, block : block + 1] * sin_ref[...]
        ).astype(BF)


def fourier_table(parts, factor):
    cos_c, sin_c, cos_f, sin_f = parts
    first = jnp.stack([factor * cos_c, -factor * sin_c], axis=1).reshape(2 * TRUNC, LANES)
    second = jnp.stack([factor * sin_c, factor * cos_c], axis=1).reshape(2 * TRUNC, LANES)
    cos_f = jnp.repeat(cos_f, 2, axis=0)
    sin_f = jnp.repeat(sin_f, 2, axis=0)
    rows = 256
    spec = pl.BlockSpec((rows, LANES), lambda i: (i, 0))
    return pl.pallas_call(
        table_kernel,
        grid=(2 * TRUNC // rows,),
        in_specs=[spec] * 4,
        out_specs=pl.BlockSpec((rows, NLON), lambda i: (i, 0)),
        out_shape=jax.ShapeDtypeStruct((2 * TRUNC, NLON), BF),
        cost_estimate=pl.CostEstimate(flops=6 * TRUNC * NLON, bytes_accessed=4 * TRUNC * NLON, transcendentals=0),
        name="fourier_table",
    )(first, second, cos_f, sin_f)


def lane_ids(shape):
    return lax.broadcasted_iota(jnp.int32, shape, len(shape) - 1)


def edge_columns_kernel(cols, tr_ref, head_ref, tail_ref, pad):
    rows = tr_ref.shape[2]
    pitch = pad.shape[1]
    pad[:, :rows, :cols] = tr_ref[0]
    flat = pad.reshape(pad.shape[0] * pitch, LANES)
    lanes = lane_ids((pad.shape[0], LANES))
    head = jnp.zeros((pad.shape[0], LANES), F32)
    tail = head
    for r in range(rows):
        line = flat[pl.ds(r, pad.shape[0], stride=pitch), :]
        here = (lanes >> 1) == r
        head = jnp.where(here, pltpu.roll(line, 2 * r, 1), head)
        tail = jnp.where(here, pltpu.roll(line, (2 * r - cols + 2) % LANES, 1), tail)
    head_ref[0] = head
    tail_ref[0] = tail


def with_columns(line, r, west, east, cols, lanes):
    line = jnp.where((lanes >> 1) == cols // 2, pltpu.roll(east, (cols - 2 * r) % LANES, 1), line)
    return jnp.where((lanes >> 1) == LANES // 2 - 1, pltpu.roll(west, (LANES - 2 - 2 * r) % LANES, 1), line)


def edge_rows_kernel(cols, tr_ref, west_ref, east_ref, top_ref, low_ref, pad):
    rows = tr_ref.shape[2]
    pitch = pad.shape[1]
    pad[:, :rows, :cols] = tr_ref[0]
    flat = pad.reshape(pad.shape[0] * pitch, LANES)
    lanes = lane_ids((pad.shape[0], LANES))
    west, east = west_ref[0], east_ref[0]
    for at, r in enumerate(range(HALO)):
        top_ref[0, at] = with_columns(flat[pl.ds(r, pad.shape[0], stride=pitch), :], r, west, east, cols, lanes)
    for at, r in enumerate(range(rows - HALO, rows)):
        low_ref[0, at] = with_columns(flat[pl.ds(r, pad.shape[0], stride=pitch), :], r, west, east, cols, lanes)


def chemistry_kernel(
    cols, total_rows, first_ref, tr_ref, north_ref, south_ref, west_ref, east_ref, u_ref, v_ref, react_ref, heat_ref,
    mix_ref, heating_ref, pad, x_ref, y_ref, coef_ref,
):
    rows = tr_ref.shape[2]
    tracers = pad.shape[0]
    pitch = pad.shape[1]
    deep = rows + 2 * HALO
    pad[:, :rows, :cols] = tr_ref[0]
    flat = pad.reshape(tracers * pitch, LANES)
    lanes = lane_ids((tracers, LANES))
    west, east = west_ref[0], east_ref[0]
    for at in range(HALO):
        x_ref[at] = north_ref[0, at]
        x_ref[rows + HALO + at] = south_ref[0, at]
    for r in range(rows):
        x_ref[HALO + r] = with_columns(flat[pl.ds(r, tracers, stride=pitch), :], r, west, east, cols, lanes)
    u, v = u_ref[0], v_ref[0]
    face_u = 0.5 * (u + pltpu.roll(u, LANES - 1, 1))
    east_up, east_down = COURANT * jnp.maximum(face_u, 0.0), COURANT * jnp.minimum(face_u, 0.0)
    face_v = 0.5 * (v + pltpu.roll(v, deep - 1, 0))
    row = first_ref[0] - HALO + lax.broadcasted_iota(jnp.int32, face_v.shape, 0)
    face_v = jnp.where((row >= 0) & (row + 1 <= total_rows - 1), face_v, 0.0)
    south_up, south_down = COURANT * jnp.maximum(face_v, 0.0), COURANT * jnp.minimum(face_v, 0.0)
    coef_ref[0] = 1.0 - east_up + pltpu.roll(east_down, 1, 1) - south_up + pltpu.roll(south_down, 1, 0)
    coef_ref[1] = -east_down
    coef_ref[2] = pltpu.roll(east_up, 1, 1)
    coef_ref[3] = -south_down
    coef_ref[4] = pltpu.roll(south_up, 1, 0)
    react = react_ref[...]

    def moved(src, r):
        q = src[r]
        return (
            coef_ref[0, r : r + 1] * q
            + coef_ref[1, r : r + 1] * pltpu.roll(q, LANES - 1, 1)
            + coef_ref[2, r : r + 1] * pltpu.roll(q, 1, 1)
            + coef_ref[3, r : r + 1] * src[r + 1]
            + coef_ref[4, r : r + 1] * src[r - 1]
        )

    def step(src, r):
        both = jnp.concatenate([moved(src, r), moved(src, r + 1)], axis=1)
        high = both.astype(BF)
        low = (both - high.astype(F32)).astype(BF)
        return both + jnp.dot(react, jnp.concatenate([high, high, low], axis=0), preferred_element_type=F32)

    for r in range(1, deep - 1, 2):
        both = step(x_ref, r)
        y_ref[r] = both[:, :LANES]
        y_ref[r + 1] = both[:, LANES:]
    heat = heat_ref[...]
    heating_ref[0] = jnp.zeros_like(heating_ref[0])
    for r in range(HALO, rows + HALO, 2):
        both = step(y_ref, r)
        for at in range(2):
            one = both[:, at * LANES : (at + 1) * LANES]
            flat[pl.ds(r - HALO + at, tracers, stride=pitch), :] = one
            heating_ref[0, r + at : r + at + 1] = jnp.sum(heat * one, axis=0, keepdims=True)
    mix_ref[0] = pad[:, :rows, :cols]


def shift(value, axis, by):
    count = lax.axis_size(axis)
    return lax.ppermute(value, axis, [(i, (i + by) % count) for i in range(count)])


def tracer_halos(tracers):
    levels, count, rows, cols = tracers.shape
    pitch = -(-rows // 8) * 8
    tr_spec = pl.BlockSpec((1, count, rows, cols), lambda l: (l, 0, 0, 0))
    col_spec = pl.BlockSpec((1, count, LANES), lambda l: (l, 0, 0))
    row_spec = pl.BlockSpec((1, HALO, count, LANES), lambda l: (l, 0, 0, 0))
    col_shape = jax.ShapeDtypeStruct((levels, count, LANES), F32)
    row_shape = jax.ShapeDtypeStruct((levels, HALO, count, LANES), F32)
    pad = [pltpu.VMEM((count, pitch, LANES), F32)]
    head, tail = pl.pallas_call(
        functools.partial(edge_columns_kernel, cols),
        grid=(levels,),
        in_specs=[tr_spec],
        out_specs=[col_spec] * 2,
        out_shape=[col_shape] * 2,
        scratch_shapes=pad,
        name="edge_columns",
    )(tracers)
    west = shift(tail, "lev", 1)
    east = shift(head, "lev", -1)
    top, low = pl.pallas_call(
        functools.partial(edge_rows_kernel, cols),
        grid=(levels,),
        in_specs=[tr_spec, col_spec, col_spec],
        out_specs=[row_spec] * 2,
        out_shape=[row_shape] * 2,
        scratch_shapes=pad,
        name="edge_rows",
    )(tracers, west, east)
    return shift(low, "wave", 1), shift(top, "wave", -1), west, east


def chemistry(tracers, halos, winds, reaction, heat_coeff, row_first, total_rows):
    levels, count, rows, cols = tracers.shape
    pitch = -(-rows // 8) * 8
    deep = rows + 2 * HALO
    high = reaction.astype(BF)
    low = (reaction - high.astype(F32)).astype(BF)
    react = jnp.concatenate([high, low, high], axis=1)
    heat = jnp.broadcast_to(heat_coeff[:, None], (count, LANES))
    tr_spec = pl.BlockSpec((1, count, rows, cols), lambda l: (l, 0, 0, 0))
    col_spec = pl.BlockSpec((1, count, LANES), lambda l: (l, 0, 0))
    row_spec = pl.BlockSpec((1, HALO, count, LANES), lambda l: (l, 0, 0, 0))
    whole = lambda shape: pl.BlockSpec(shape, lambda l: (0,) * len(shape))
    return pl.pallas_call(
        functools.partial(chemistry_kernel, cols, total_rows),
        grid=(levels,),
        in_specs=[
            pl.BlockSpec(memory_space=pltpu.SMEM),
            tr_spec,
            row_spec,
            row_spec,
            col_spec,
            col_spec,
            pl.BlockSpec((1, deep, LANES), lambda l: (l, 0, 0)),
            pl.BlockSpec((1, deep, LANES), lambda l: (l + levels, 0, 0)),
            whole(react.shape),
            whole(heat.shape),
        ],
        out_specs=[tr_spec, pl.BlockSpec((1, deep, LANES), lambda l: (l, 0, 0))],
        out_shape=[
            jax.ShapeDtypeStruct(tracers.shape, F32),
            jax.ShapeDtypeStruct((levels, deep, LANES), F32),
        ],
        scratch_shapes=[
            pltpu.VMEM((count, pitch, LANES), F32),
            pltpu.VMEM((deep, count, LANES), F32),
            pltpu.VMEM((deep, count, LANES), F32),
            pltpu.VMEM((5, deep, LANES), F32),
        ],
        cost_estimate=pl.CostEstimate(flops=10**9, bytes_accessed=16 * 10**6, transcendentals=0),
        name="chemistry",
    )(row_first.reshape(1), tracers, *halos, winds, winds, react, heat)


def body(spectra, legendre, gauss_weights, phys_matrix, phys_bias, tracers, reaction, heat_coeff):
    waves = lax.axis_size("wave")
    levs = lax.axis_size("lev")
    both = ("wave", "lev")
    wave, lev = lax.axis_index("wave"), lax.axis_index("lev")
    m_count, k_count, _, fields = spectra.shape
    half_rows = legendre.shape[1]
    levels, _, chem_rows, chem_cols = tracers.shape
    ratio = NLON // (chem_cols * levs)
    bands = waves // 2
    band_rows = half_rows // bands
    edge = ratio * HALO
    groups = (chem_rows + 2 * HALO) // levs
    deep = band_rows + 2 * edge
    south = wave >= bands
    width = 2 * fields

    halos = tracer_halos(tracers)
    parts = angle_parts()
    m_all = jnp.arange(TRUNC, dtype=jnp.int32)[:, None]
    inverse = fourier_table(parts, jnp.where(m_all == 0, 1.0, 2.0).astype(F32))
    direct = fourier_table(parts, jnp.full((TRUNC, 1), 1.0 / math.sqrt(NLON), F32))

    m_local = (wave * levs + lev) * m_count + jnp.arange(m_count, dtype=jnp.int32)
    k_index = jnp.arange(k_count, dtype=jnp.int32)
    keep_mask = spectral_keep(m_local, k_index)
    masked = jnp.where(keep_mask[..., None], spectra, jnp.zeros_like(spectra)).reshape(m_count, k_count, width)
    parity = jnp.where(k_index % 2 == 0, 1.0, -1.0).astype(BF)
    stacked = jnp.concatenate([masked, masked * parity[None, :, None]], axis=2)
    project = jnp.einsum("mik,mkx->mix", legendre, stacked, preferred_element_type=F32).astype(BF)
    north, south_part = project[:, :, :width], project[:, :, width:]
    blank = jnp.zeros((m_count, edge, width), BF)

    def windows(mine, other):
        padded = jnp.concatenate([blank, mine, jnp.flip(other[:, half_rows - edge :], axis=1)], axis=1)
        return [padded[:, b * band_rows : b * band_rows + deep] for b in range(bands)]

    pieces = jnp.stack(windows(north, south_part) + windows(south_part, north)[::-1])
    pieces = pieces.reshape(waves, m_count, levs, groups, ratio, 2, fields).transpose(0, 2, 3, 1, 5, 4, 6)
    pieces = pieces.reshape(waves * levs, groups * m_count * 2, ratio * fields)
    spread = lax.all_to_all(pieces, both, split_axis=0, concat_axis=0, tiled=True)
    spread = spread.reshape(waves * levs, groups, 2 * m_count, ratio * fields).transpose(0, 2, 1, 3)
    spread = spread.reshape(2 * TRUNC, groups * ratio * fields)

    grid = lax.dot_general(spread, inverse, (((0,), (0,)), ((), ())), preferred_element_type=F32).astype(BF)
    grid = grid.reshape(groups, ratio, fields, NLON)

    lane = jnp.arange(LANES, dtype=jnp.int32)
    column = jnp.where(lane < LANES - HALO, lane, lane - LANES)
    column = (column[None, :] + chem_cols * jnp.arange(levs, dtype=jnp.int32)[:, None]) % (chem_cols * levs)
    used = (lane < chem_cols + HALO) | (lane >= LANES - HALO)
    column = jnp.where(used[None, :], column, -1).reshape(levs * LANES)
    cell = jnp.arange(NLON, dtype=jnp.int32) // ratio
    mean = jnp.where(cell[:, None] == column[None, :], 1.0 / ratio**2, 0.0).astype(BF)
    winds = jnp.einsum("gqfj,jx->gfx", grid[:, :, : 2 * levels], mean, preferred_element_type=F32)
    winds = winds.reshape(groups * 2 * levels, levs, LANES).transpose(1, 0, 2)
    winds = lax.all_to_all(winds, "lev", split_axis=0, concat_axis=0, tiled=True)
    winds = winds.reshape(levs * groups, 2 * levels, LANES)
    winds = jnp.where(south, jnp.flip(winds, axis=0), winds).transpose(1, 0, 2)

    mixing, heating = chemistry(
        tracers, halos, winds, reaction, heat_coeff, wave * chem_rows, chem_rows * waves
    )
    heating = heating.transpose(1, 0, 2)
    heating = jnp.where(south, jnp.flip(heating, axis=0), heating).reshape(levs, groups * levels, LANES)
    heating = lax.all_to_all(heating, "lev", split_axis=0, concat_axis=0, tiled=True)
    heating = heating.reshape(levs, groups, levels, LANES)[..., :chem_cols].transpose(1, 2, 0, 3)
    heating = jnp.repeat(heating.reshape(groups, 1, levels, levs * chem_cols), ratio, axis=3)

    physics = jnp.tanh(
        jnp.einsum("ef,gqfj->gqej", phys_matrix, grid.astype(F32), precision=lax.Precision.HIGHEST)
        + phys_bias[:, None]
    )
    tendency = jnp.concatenate(
        [physics[:, :, : 2 * levels], physics[:, :, 2 * levels : 3 * levels] + heating, physics[:, :, 3 * levels :]],
        axis=2,
    ).astype(BF)

    tendency = tendency.reshape(groups * ratio * fields, NLON)
    coeffs = lax.dot_general(direct, tendency, (((1,), (1,)), ((), ())), preferred_element_type=F32).astype(BF)
    coeffs = coeffs.reshape(waves * levs, 2 * m_count, groups, ratio * fields).transpose(0, 2, 1, 3)
    coeffs = coeffs.reshape(waves * levs, groups * 2 * m_count, ratio * fields)
    values = lax.all_to_all(coeffs, both, split_axis=0, concat_axis=0, tiled=True)

    values = values.reshape(waves, levs, groups, m_count, 2, ratio, fields)
    values = values.transpose(3, 0, 1, 2, 5, 4, 6).reshape(m_count, waves, deep, width)[:, :, edge : edge + band_rows]
    north = values[:, :bands].reshape(m_count, half_rows, width).astype(F32)
    south_part = jnp.flip(values[:, bands:], axis=1).reshape(m_count, half_rows, width).astype(F32)
    weights = gauss_weights[None, :, None]
    paired = jnp.concatenate([weights * (north + south_part), weights * (north - south_part)], axis=2).astype(BF)
    folded = jnp.einsum("mik,mix->mkx", legendre, paired, preferred_element_type=F32)
    even_rows = (k_index % 2 == 0)[None, :, None]
    chosen = jnp.where(even_rows, folded[:, :, :width], folded[:, :, width:]).reshape(m_count, k_count, 2, fields)
    result = jnp.where(keep_mask[..., None], chosen, 0.0).astype(BF)
    return (result, mixing)


def solution(mesh):
    return jax.shard_map(
        body,
        mesh=mesh,
        in_specs=(
            P(("wave", "lev"), None, None, None),
            P(("wave", "lev"), None, None),
            P(),
            P(),
            P(),
            P(None, None, "wave", "lev"),
            P(),
            P(),
        ),
        out_specs=(P(("wave", "lev"), None, None, None), P(None, None, "wave", "lev")),
        check_vma=False,
    )
```

```python
import functools
import math

import jax
import jax.numpy as jnp
from jax import lax
from jax.experimental import pallas as pl
from jax.experimental.pallas import tpu as pltpu
from jax.sharding import PartitionSpec as P

TRUNC = 1280
NLON = 2560
SUBSTEPS = 2
COURANT = 0.6
LANES = 128
PIECE_ROWS = 64
HALO = 2
BF, F32 = jnp.bfloat16, jnp.float32


TABLE_ROWS = 160


def table_kernel(cos_ref, sin_ref, sign_ref, a_ref, b_ref, inverse_ref, direct_ref):
    rows = cos_ref.shape[0]
    cos, sin, sign = cos_ref[...], sin_ref[...], sign_ref[...]
    first = (lax.broadcasted_iota(jnp.int32, cos.shape, 0) == 0) & (pl.program_id(0) == 0)
    factor = jnp.where(first, 1.0, 2.0)
    scale = 1.0 / math.sqrt(NLON)
    for block in range(NLON // LANES):
        part = slice(block * LANES, (block + 1) * LANES)
        value = cos * a_ref[:, part] - sin * b_ref[:, part]
        if block % 2:
            value = value * sign
        inverse_ref[:, part] = (value * factor).astype(BF)
        direct_ref[:, part] = (value * scale).astype(BF)


def fourier_tables(owners, m_count):
    unit = 2.0 * math.pi / NLON
    owner = jnp.arange(owners, dtype=jnp.int32)
    lane = jnp.arange(LANES, dtype=jnp.int32)
    coarse = (m_count * owner[:, None] * lane[None, :] % NLON).astype(F32) * unit
    sign = jnp.where(owner % 2 == 1, -1.0, 1.0).astype(F32)[:, None]
    rows = 2 * m_count
    per_row = lambda value: jnp.broadcast_to(value[:, None, :], (owners, rows, LANES)).reshape(-1, LANES)
    inner = jnp.arange(m_count, dtype=jnp.int32)[:, None]
    fine = (inner * jnp.arange(NLON, dtype=jnp.int32)[None, :] % NLON).astype(F32) * unit
    cos, sin = jnp.cos(fine), jnp.sin(fine)
    repeat = TABLE_ROWS // rows
    a = jnp.tile(jnp.concatenate([cos, -sin]), (repeat, 1))
    b = jnp.tile(jnp.concatenate([sin, cos]), (repeat, 1))
    row_spec = pl.BlockSpec((TABLE_ROWS, LANES), lambda i: (i, 0))
    all_spec = pl.BlockSpec((TABLE_ROWS, NLON), lambda i: (0, 0))
    out_spec = pl.BlockSpec((TABLE_ROWS, NLON), lambda i: (i, 0))
    shape = jax.ShapeDtypeStruct((owners * rows, NLON), BF)
    return pl.pallas_call(
        table_kernel,
        grid=(owners * rows // TABLE_ROWS,),
        in_specs=[row_spec] * 3 + [all_spec] * 2,
        out_specs=[out_spec] * 2,
        out_shape=[shape] * 2,
        cost_estimate=pl.CostEstimate(flops=12 * TRUNC * NLON, bytes_accessed=8 * TRUNC * NLON, transcendentals=0),
        name="fourier_tables",
    )(per_row(jnp.cos(coarse)), per_row(jnp.sin(coarse)), per_row(jnp.broadcast_to(sign, coarse.shape)), a, b)


def swapped(x):
    shape = x.shape
    x = x.reshape(-1, 8, LANES)
    row = lax.broadcasted_iota(jnp.int32, x.shape, 1)
    block = lax.broadcasted_iota(jnp.int32, x.shape, 2) // 32
    for bit in (2, 1):
        span = 32 * bit
        low, high = (row & bit) == 0, (block & bit) == 0
        from_below = pltpu.roll(pltpu.roll(x, 8 - bit, 1), span, 2)
        from_above = pltpu.roll(pltpu.roll(x, bit, 1), LANES - span, 2)
        x = jnp.where(low == high, x, jnp.where(low, from_below, from_above))
    return x.reshape(shape)


def kept(m, shape, part_rows):
    row = lax.broadcasted_iota(jnp.int32, shape, 0)
    k = lax.broadcasted_iota(jnp.int32, shape, 1)
    return (k < TRUNC - m) & ((row < part_rows) | (m > 0)), k % 2 == 0


def inverse_kernel(geometry, first_ref, spec_ref, leg_ref, out_ref, z_ref, q_ref):
    waves, levs, groups, bands, band_groups, m_count = geometry
    half_rows = leg_ref.shape[1]
    step = pl.program_id(0)
    spec = spec_ref[0].astype(F32)
    keep, even = kept(first_ref[0] + step, spec.shape, spec.shape[0] // 2)
    spec = jnp.where(keep, spec, 0.0)
    stacked = jnp.concatenate([spec, jnp.where(even, spec, -spec)], axis=0).astype(BF)
    values = lax.dot_general(leg_ref[0], stacked, (((1,), (1,)), ((), ())), preferred_element_type=F32)
    z_ref[pl.ds(step * half_rows, half_rows), :] = swapped(values)

    @pl.when(step == m_count - 1)
    def _():
        q_ref[...] = jnp.zeros_like(q_ref)

        def of_wave(wave, carry):
            south = (wave >= bands).astype(jnp.int32)
            band = jnp.where(wave >= bands, waves - 1 - wave, wave)
            for lev in range(levs):
                for g in range(groups):
                    at = band * band_groups + (lev * groups + g - HALO)
                    over = at >= bands * band_groups
                    line = jnp.where(over, 2 * bands * band_groups - 1 - at, jnp.maximum(at, 0))
                    base = line * 4 + jnp.where(over, 1 - south, south) * 2
                    for c in range(2):
                        row = (g * 2 + c) * m_count
                        q_ref[lev, row : row + m_count] = z_ref[pl.ds(base + c, m_count, stride=half_rows), :]
                out_ref[wave * levs + lev] = q_ref[lev].astype(BF)
            return carry

        lax.fori_loop(0, waves, of_wave, 0)


def direct_kernel(geometry, first_ref, values_ref, weights_ref, leg_ref, out_ref, z_ref, q_ref):
    waves, levs, groups, bands, band_groups, m_count = geometry
    half_rows = leg_ref.shape[1]
    step = pl.program_id(0)

    @pl.when(step == 0)
    def _():
        def of_wave(wave, carry):
            south = (wave >= bands).astype(jnp.int32)
            band = jnp.where(wave >= bands, waves - 1 - wave, wave)
            for lev in range(levs):
                q_ref[lev] = values_ref[wave * levs + lev].astype(F32)
                for g in range(groups):
                    inside = lev * groups + g - HALO
                    if 0 <= inside < band_groups:
                        base = (band * band_groups + inside) * 4 + south * 2
                        for c in range(2):
                            row = (g * 2 + c) * m_count
                            z_ref[pl.ds(base + c, m_count, stride=half_rows), :] = q_ref[lev, row : row + m_count]
            return carry

        lax.fori_loop(0, waves, of_wave, 0)

    x = swapped(z_ref[pl.ds(step * half_rows, half_rows), :])
    y = pltpu.roll(x, LANES // 2, 1)
    north = lane_ids(x.shape) < LANES // 2
    paired = (weights_ref[...] * jnp.where(north, x + y, y - x)).astype(BF)
    folded = lax.dot_general(paired, leg_ref[0], (((0,), (0,)), ((), ())), preferred_element_type=F32)
    half = folded.shape[0] // 2
    keep, even = kept(first_ref[0] + step, (half, folded.shape[1]), half // 2)
    chosen = jnp.where(even, folded[:half], folded[half:])
    out_ref[0] = jnp.where(keep, chosen, 0.0).astype(BF)


def legendre_call(kernel, name, first, operands, in_specs, out_spec, out_shape, geometry, legendre):
    m_count, half_rows, k_count = legendre.shape
    levs = geometry[1]
    return pl.pallas_call(
        functools.partial(kernel, geometry),
        grid=(m_count,),
        in_specs=[pl.BlockSpec(memory_space=pltpu.SMEM)]
        + in_specs
        + [pl.BlockSpec((1, half_rows, k_count), lambda m: (m, 0, 0))],
        out_specs=out_spec,
        out_shape=out_shape,
        scratch_shapes=[
            pltpu.VMEM((m_count * half_rows, LANES), F32),
            pltpu.VMEM((levs, PIECE_ROWS, LANES), F32),
        ],
        cost_estimate=pl.CostEstimate(
            flops=2 * legendre.size * LANES, bytes_accessed=2 * legendre.size + 5 * 10**6, transcendentals=0
        ),
        name=name,
    )(first.reshape(1), *operands, legendre)


def lane_ids(shape):
    return lax.broadcasted_iota(jnp.int32, shape, len(shape) - 1)


def edge_columns_kernel(tr_ref, head_ref, tail_ref, pad):
    rows, count, cols = tr_ref.shape[1:]
    lanes = lane_ids((count, LANES))
    head = jnp.zeros((count, LANES), F32)
    tail = head
    pad[:, :, :cols] = tr_ref[0]
    for r in range(rows):
        line = pad[r]
        here = (lanes >> 1) == r
        head = jnp.where(here, pltpu.roll(line, 2 * r, 1), head)
        tail = jnp.where(here, pltpu.roll(line, (2 * r - cols + 2) % LANES, 1), tail)
    head_ref[0] = head
    tail_ref[0] = tail


def with_columns(line, r, west, east, cols, lanes):
    line = jnp.where((lanes >> 1) == cols // 2, pltpu.roll(east, (cols - 2 * r) % LANES, 1), line)
    return jnp.where((lanes >> 1) == LANES // 2 - 1, pltpu.roll(west, (LANES - 2 - 2 * r) % LANES, 1), line)


def edge_rows_kernel(rows, first_ref, last_ref, west_ref, east_ref, top_ref, low_ref):
    count, cols = first_ref.shape[2:]
    lanes = lane_ids((count, LANES))
    west, east = west_ref[0], east_ref[0]
    for at in range(HALO):
        for src, out, r in ((first_ref, top_ref, at), (last_ref, low_ref, rows - HALO + at)):
            out[0, at, :, :cols] = src[0, at]
            out[0, at] = with_columns(out[0, at], r, west, east, cols, lanes)


def chemistry_kernel(
    total_rows, first_ref, tr_ref, north_ref, south_ref, west_ref, east_ref, u_ref, v_ref, react_ref, heat_ref,
    mix_ref, heating_ref, x_ref, y_ref, coef_ref,
):
    rows, tracers, cols = tr_ref.shape[1:]
    deep = rows + 2 * HALO
    lanes = lane_ids((tracers, LANES))
    west, east = west_ref[0], east_ref[0]
    for at in range(HALO):
        x_ref[at] = north_ref[0, at]
        x_ref[rows + HALO + at] = south_ref[0, at]
    x_ref[HALO : HALO + rows, :, :cols] = tr_ref[0]
    for r in range(rows):
        x_ref[HALO + r] = with_columns(x_ref[HALO + r], r, west, east, cols, lanes)
    u, v = u_ref[0], v_ref[0]
    face_u = 0.5 * (u + pltpu.roll(u, LANES - 1, 1))
    east_up, east_down = COURANT * jnp.maximum(face_u, 0.0), COURANT * jnp.minimum(face_u, 0.0)
    face_v = 0.5 * (v + pltpu.roll(v, deep - 1, 0))
    row = first_ref[0] - HALO + lax.broadcasted_iota(jnp.int32, face_v.shape, 0)
    face_v = jnp.where((row >= 0) & (row + 1 <= total_rows - 1), face_v, 0.0)
    south_up, south_down = COURANT * jnp.maximum(face_v, 0.0), COURANT * jnp.minimum(face_v, 0.0)
    coef_ref[0] = 1.0 - east_up + pltpu.roll(east_down, 1, 1) - south_up + pltpu.roll(south_down, 1, 0)
    coef_ref[1] = -east_down
    coef_ref[2] = pltpu.roll(east_up, 1, 1)
    coef_ref[3] = -south_down
    coef_ref[4] = pltpu.roll(south_up, 1, 0)
    react = react_ref[...]

    def moved(src, r):
        q = src[r]
        return (
            coef_ref[0, r : r + 1] * q
            + coef_ref[1, r : r + 1] * pltpu.roll(q, LANES - 1, 1)
            + coef_ref[2, r : r + 1] * pltpu.roll(q, 1, 1)
            + coef_ref[3, r : r + 1] * src[r + 1]
            + coef_ref[4, r : r + 1] * src[r - 1]
        )

    def step(src, r):
        both = jnp.concatenate([moved(src, r), moved(src, r + 1)], axis=1)
        high = both.astype(BF)
        low = (both - high.astype(F32)).astype(BF)
        return both + jnp.dot(react, jnp.concatenate([high, high, low], axis=0), preferred_element_type=F32)

    for r in range(1, deep - 1, 2):
        both = step(x_ref, r)
        y_ref[r] = both[:, :LANES]
        y_ref[r + 1] = both[:, LANES:]
    heat = heat_ref[...]
    heating_ref[0] = jnp.zeros_like(heating_ref[0])
    for r in range(HALO, rows + HALO, 2):
        both = step(y_ref, r)
        for at in range(2):
            one = both[:, at * LANES : (at + 1) * LANES]
            mix_ref[0, r - HALO + at] = one[:, :cols]
            heating_ref[0, r + at : r + at + 1] = jnp.sum(heat * one, axis=0, keepdims=True)


def shift(value, axis, by):
    count = lax.axis_size(axis)
    return lax.ppermute(value, axis, [(i, (i + by) % count) for i in range(count)])


def tracer_halos(tracers):
    levels, rows, count, cols = tracers.shape
    tr_spec = pl.BlockSpec((1, rows, count, cols), lambda l: (l, 0, 0, 0))
    col_spec = pl.BlockSpec((1, count, LANES), lambda l: (l, 0, 0))
    row_spec = pl.BlockSpec((1, HALO, count, LANES), lambda l: (l, 0, 0, 0))
    col_shape = jax.ShapeDtypeStruct((levels, count, LANES), F32)
    row_shape = jax.ShapeDtypeStruct((levels, HALO, count, LANES), F32)
    head, tail = pl.pallas_call(
        edge_columns_kernel,
        grid=(levels,),
        in_specs=[tr_spec],
        out_specs=[col_spec] * 2,
        out_shape=[col_shape] * 2,
        scratch_shapes=[pltpu.VMEM((rows, count, LANES), F32)],
        cost_estimate=pl.CostEstimate(flops=10**7, bytes_accessed=7 * 10**6, transcendentals=0),
        name="edge_columns",
    )(tracers)
    west = shift(tail, "lev", 1)
    east = shift(head, "lev", -1)
    top, low = pl.pallas_call(
        functools.partial(edge_rows_kernel, rows),
        grid=(levels,),
        in_specs=[
            pl.BlockSpec((1, HALO, count, cols), lambda l: (l, 0, 0, 0)),
            pl.BlockSpec((1, HALO, count, cols), lambda l: (l, rows // HALO - 1, 0, 0)),
            col_spec,
            col_spec,
        ],
        out_specs=[row_spec] * 2,
        out_shape=[row_shape] * 2,
        cost_estimate=pl.CostEstimate(flops=10**6, bytes_accessed=2 * 10**6, transcendentals=0),
        name="edge_rows",
    )(tracers, tracers, west, east)
    return shift(low, "wave", 1), shift(top, "wave", -1), west, east


def chemistry(tracers, halos, winds, reaction, heat_coeff, row_first, total_rows):
    levels, rows, count, cols = tracers.shape
    deep = rows + 2 * HALO
    high = reaction.astype(BF)
    low = (reaction - high.astype(F32)).astype(BF)
    react = jnp.concatenate([high, low, high], axis=1)
    heat = jnp.broadcast_to(heat_coeff[:, None], (count, LANES))
    tr_spec = pl.BlockSpec((1, rows, count, cols), lambda l: (l, 0, 0, 0))
    col_spec = pl.BlockSpec((1, count, LANES), lambda l: (l, 0, 0))
    row_spec = pl.BlockSpec((1, HALO, count, LANES), lambda l: (l, 0, 0, 0))
    whole = lambda shape: pl.BlockSpec(shape, lambda l: (0,) * len(shape))
    return pl.pallas_call(
        functools.partial(chemistry_kernel, total_rows),
        grid=(levels,),
        in_specs=[
            pl.BlockSpec(memory_space=pltpu.SMEM),
            tr_spec,
            row_spec,
            row_spec,
            col_spec,
            col_spec,
            pl.BlockSpec((1, deep, LANES), lambda l: (l, 0, 0)),
            pl.BlockSpec((1, deep, LANES), lambda l: (l + levels, 0, 0)),
            whole(react.shape),
            whole(heat.shape),
        ],
        out_specs=[tr_spec, pl.BlockSpec((1, deep, LANES), lambda l: (l, 0, 0))],
        out_shape=[
            jax.ShapeDtypeStruct(tracers.shape, F32),
            jax.ShapeDtypeStruct((levels, deep, LANES), F32),
        ],
        scratch_shapes=[
            pltpu.VMEM((deep, count, LANES), F32),
            pltpu.VMEM((deep, count, LANES), F32),
            pltpu.VMEM((5, deep, LANES), F32),
        ],
        cost_estimate=pl.CostEstimate(flops=10**9, bytes_accessed=16 * 10**6, transcendentals=0),
        name="chemistry",
    )(row_first.reshape(1), tracers, *halos, winds, winds, react, heat)


def body(spectra, legendre, gauss_weights, phys_matrix, phys_bias, tracers, reaction, heat_coeff):
    waves = lax.axis_size("wave")
    levs = lax.axis_size("lev")
    both = ("wave", "lev")
    wave, lev = lax.axis_index("wave"), lax.axis_index("lev")
    m_count, k_count, _, fields = spectra.shape
    half_rows = legendre.shape[1]
    levels, _, chem_rows, chem_cols = tracers.shape
    ratio = NLON // (chem_cols * levs)
    bands = waves // 2
    groups = (chem_rows + 2 * HALO) // levs
    south = wave >= bands
    width = 2 * fields

    owners = waves * levs
    geometry = (waves, levs, groups, bands, chem_rows, m_count)
    first_m = (wave * levs + lev) * m_count
    piece_shape = (owners, PIECE_ROWS, LANES)
    piece_spec = pl.BlockSpec(piece_shape, lambda m: (0, 0, 0))
    spec_spec = pl.BlockSpec((1, width, k_count), lambda m: (m, 0, 0))
    used = groups * 2 * m_count
    tracers = tracers.transpose(0, 2, 1, 3)

    pieces = legendre_call(
        inverse_kernel,
        "to_latitude",
        first_m,
        [spectra.transpose(0, 2, 3, 1).reshape(m_count, width, k_count)],
        [spec_spec],
        piece_spec,
        jax.ShapeDtypeStruct(piece_shape, BF),
        geometry,
        legendre,
    )
    spread = lax.all_to_all(pieces, both, split_axis=0, concat_axis=0, tiled=True)
    halos = tracer_halos(tracers)
    inverse, direct = fourier_tables(owners, m_count)
    spread = spread[:, :used].reshape(owners, groups, 2 * m_count, LANES).transpose(0, 2, 1, 3)
    spread = spread.reshape(2 * TRUNC, groups * LANES)

    grid = lax.dot_general(spread, inverse, (((0,), (0,)), ((), ())), preferred_element_type=F32).astype(BF)
    grid = grid.reshape(groups, ratio, fields, NLON)

    lane = jnp.arange(LANES, dtype=jnp.int32)
    column = jnp.where(lane < LANES - HALO, lane, lane - LANES)
    column = (column[None, :] + chem_cols * jnp.arange(levs, dtype=jnp.int32)[:, None]) % (chem_cols * levs)
    held = (lane < chem_cols + HALO) | (lane >= LANES - HALO)
    column = jnp.where(held[None, :], column, -1).reshape(levs * LANES)
    cell = jnp.arange(NLON, dtype=jnp.int32) // ratio
    mean = jnp.where(cell[:, None] == column[None, :], 1.0 / ratio**2, 0.0).astype(BF)
    winds = jnp.einsum("gqfj,jx->gfx", grid[:, :, : 2 * levels], mean, preferred_element_type=F32)
    winds = winds.reshape(groups * 2 * levels, levs, LANES).transpose(1, 0, 2)
    winds = lax.all_to_all(winds, "lev", split_axis=0, concat_axis=0, tiled=True)
    winds = winds.reshape(levs * groups, 2 * levels, LANES)
    winds = jnp.where(south, jnp.flip(winds, axis=0), winds).transpose(1, 0, 2)

    mixing, heating = chemistry(
        tracers, halos, winds, reaction, heat_coeff, wave * chem_rows, chem_rows * waves
    )
    heating = heating.transpose(1, 0, 2)
    heating = jnp.where(south, jnp.flip(heating, axis=0), heating).reshape(levs, groups * levels, LANES)
    heating = lax.all_to_all(heating, "lev", split_axis=0, concat_axis=0, tiled=True)
    heating = heating.reshape(levs, groups, levels, LANES)[..., :chem_cols].transpose(1, 2, 0, 3)
    heating = jnp.repeat(heating.reshape(groups, 1, levels, levs * chem_cols), ratio, axis=3)

    physics = jnp.tanh(
        jnp.einsum("ef,gqfj->gqej", phys_matrix, grid.astype(F32), precision=lax.Precision.HIGHEST)
        + phys_bias[:, None]
    )
    tendency = jnp.concatenate(
        [physics[:, :, : 2 * levels], physics[:, :, 2 * levels : 3 * levels] + heating, physics[:, :, 3 * levels :]],
        axis=2,
    ).astype(BF)

    tendency = tendency.reshape(groups * ratio * fields, NLON)
    coeffs = lax.dot_general(direct, tendency, (((1,), (1,)), ((), ())), preferred_element_type=F32).astype(BF)
    coeffs = coeffs.reshape(owners, 2 * m_count, groups, LANES).transpose(0, 2, 1, 3).reshape(owners, used, LANES)
    coeffs = jnp.pad(coeffs, ((0, 0), (0, PIECE_ROWS - used), (0, 0)))
    values = lax.all_to_all(coeffs, both, split_axis=0, concat_axis=0, tiled=True)

    result = legendre_call(
        direct_kernel,
        "to_spectral",
        first_m,
        [values, jnp.broadcast_to(gauss_weights[:, None], (half_rows, LANES))],
        [piece_spec, pl.BlockSpec((half_rows, LANES), lambda m: (0, 0))],
        spec_spec,
        jax.ShapeDtypeStruct((m_count, width, k_count), BF),
        geometry,
        legendre,
    )
    result = result.reshape(m_count, 2, fields, k_count).transpose(0, 3, 1, 2)
    mixing = mixing.transpose(0, 2, 1, 3)
    return (result, mixing)


def solution(mesh):
    return jax.shard_map(
        body,
        mesh=mesh,
        in_specs=(
            P(("wave", "lev"), None, None, None),
            P(("wave", "lev"), None, None),
            P(),
            P(),
            P(),
            P(None, None, "wave", "lev"),
            P(),
            P(),
        ),
        out_specs=(P(("wave", "lev"), None, None, None), P(None, None, "wave", "lev")),
        check_vma=False,
    )
```

```python
import functools
import math

import jax
import jax.numpy as jnp
from jax import lax
from jax.experimental import pallas as pl
from jax.experimental.pallas import tpu as pltpu
from jax.sharding import PartitionSpec as P

TRUNC = 1280
NLON = 2560
SUBSTEPS = 2
COURANT = 0.6
LANES = 128
PIECE_ROWS = 64
HALO = 2
BF, F32 = jnp.bfloat16, jnp.float32


def table_kernel(cos_ref, sin_ref, turned_cos_ref, turned_sin_ref, a_ref, b_ref, inverse_ref, direct_ref):
    step = pl.program_id(0)
    scale = 1.0 / math.sqrt(NLON)
    for block in range(NLON // LANES):
        part = slice(block * LANES, (block + 1) * LANES)
        cos, sin = (turned_cos_ref, turned_sin_ref) if block % 2 else (cos_ref, sin_ref)
        value = cos[...] * a_ref[0, :, part] - sin[...] * b_ref[0, :, part]
        inverse_ref[:, part] = (value + value).astype(BF)
        direct_ref[:, part] = (value * scale).astype(BF)

    @pl.when(step == 0)
    def _():
        top = inverse_ref[:16, :].astype(F32)
        first = lax.broadcasted_iota(jnp.int32, top.shape, 0) == 0
        inverse_ref[:16, :] = jnp.where(first, 0.5 * top, top).astype(BF)


def fourier_tables(owners, m_count):
    unit = 2.0 * math.pi / NLON
    owner = jnp.arange(owners, dtype=jnp.int32)[:, None]
    lane = jnp.arange(LANES, dtype=jnp.int32)[None, :]
    coarse = (m_count * owner * lane % NLON).astype(F32) * unit
    cos_c, sin_c = jnp.cos(coarse), jnp.sin(coarse)
    turn = jnp.where(owner % 2 == 1, -1.0, 1.0).astype(F32)
    inner = jnp.arange(m_count, dtype=jnp.int32)[:, None]
    fine = (inner * jnp.arange(NLON, dtype=jnp.int32)[None, :] % NLON).astype(F32) * unit
    cos, sin = jnp.cos(fine), jnp.sin(fine)
    a = jnp.concatenate([cos, -sin])
    b = jnp.concatenate([sin, cos])
    rows = 2 * m_count
    coarse_spec = pl.BlockSpec((owners, LANES), lambda i: (0, 0))
    fine_spec = pl.BlockSpec((1, 1, NLON), lambda i: (i, 0, 0))
    out_spec = pl.BlockSpec((owners, NLON), lambda i: (i, 0))
    shape = jax.ShapeDtypeStruct((owners * rows, NLON), BF)
    return pl.pallas_call(
        table_kernel,
        grid=(rows,),
        in_specs=[coarse_spec] * 4 + [fine_spec] * 2,
        out_specs=[out_spec] * 2,
        out_shape=[shape] * 2,
        cost_estimate=pl.CostEstimate(flops=12 * TRUNC * NLON, bytes_accessed=8 * TRUNC * NLON, transcendentals=0),
        name="fourier_tables",
    )(cos_c, sin_c, turn * cos_c, turn * sin_c, a[:, None], b[:, None])


def exchanged(x, turned):
    lanes = lane_ids(x[0].shape)
    low, even = lanes < 64, (lanes & 32) == 0
    pairs = [(jnp.where(low, x[i], turned[i + 2]), jnp.where(low, turned[i], x[i + 2])) for i in range(2)]
    out = []
    for first, second in zip(*pairs):
        out.append(jnp.where(even, first, pltpu.roll(second, 32, 1)))
        out.append(jnp.where(even, pltpu.roll(first, LANES - 32, 1), second))
    return out


def kept(m, shape, part_rows):
    row = lax.broadcasted_iota(jnp.int32, shape, 0)
    k = lax.broadcasted_iota(jnp.int32, shape, 1)
    return (k < TRUNC - m) & ((row < part_rows) | (m > 0)), k % 2 == 0


def inverse_kernel(geometry, first_ref, spec_ref, leg_ref, out_ref, z_ref, q_ref, x_ref, turned_ref):
    waves, levs, groups, bands, band_groups, m_count = geometry
    half_rows = leg_ref.shape[1]
    step = pl.program_id(0)
    spec = spec_ref[0].astype(F32)
    keep, even = kept(first_ref[0] + step, spec.shape, spec.shape[0] // 2)
    spec = jnp.where(keep, spec, 0.0)
    other = jnp.where(even, spec, -spec)
    stacked = jnp.concatenate([spec, other, other, spec], axis=0).astype(BF)
    values = lax.dot_general(leg_ref[0], stacked, (((1,), (1,)), ((), ())), preferred_element_type=F32)
    x_ref[...] = values[:, :LANES]
    turned_ref[...] = values[:, LANES:]
    quarter = half_rows // 4
    lines = [pl.ds(q, quarter, stride=4) for q in range(4)]
    for part, value in enumerate(exchanged([x_ref[i, :] for i in lines], [turned_ref[i, :] for i in lines])):
        z_ref[pl.ds(step * half_rows + part * quarter, quarter), :] = value

    @pl.when(step == m_count - 1)
    def _():
        q_ref[...] = jnp.zeros_like(q_ref)

        def of_wave(wave, carry):
            south = (wave >= bands).astype(jnp.int32)
            band = jnp.where(wave >= bands, waves - 1 - wave, wave)
            for lev in range(levs):
                for g in range(groups):
                    at = band * band_groups + (lev * groups + g - HALO)
                    over = at >= bands * band_groups
                    line = jnp.where(over, 2 * bands * band_groups - 1 - at, jnp.maximum(at, 0))
                    base = line + jnp.where(over, 1 - south, south) * (half_rows // 2)
                    for c in range(2):
                        row = (g * 2 + c) * m_count
                        start = base + c * (half_rows // 4)
                        q_ref[lev, row : row + m_count] = z_ref[pl.ds(start, m_count, stride=half_rows), :]
                out_ref[wave * levs + lev] = q_ref[lev].astype(BF)
            return carry

        lax.fori_loop(0, waves, of_wave, 0)


def direct_kernel(geometry, first_ref, values_ref, weights_ref, leg_ref, out_ref, z_ref, q_ref, x_ref):
    waves, levs, groups, bands, band_groups, m_count = geometry
    half_rows = leg_ref.shape[1]
    step = pl.program_id(0)

    @pl.when(step == 0)
    def _():
        def of_wave(wave, carry):
            south = (wave >= bands).astype(jnp.int32)
            band = jnp.where(wave >= bands, waves - 1 - wave, wave)
            for lev in range(levs):
                q_ref[lev] = values_ref[wave * levs + lev].astype(F32)
                for g in range(groups):
                    inside = lev * groups + g - HALO
                    if 0 <= inside < band_groups:
                        base = band * band_groups + inside + south * (half_rows // 2)
                        for c in range(2):
                            row = (g * 2 + c) * m_count
                            start = base + c * (half_rows // 4)
                            z_ref[pl.ds(start, m_count, stride=half_rows), :] = q_ref[lev, row : row + m_count]
            return carry

        lax.fori_loop(0, waves, of_wave, 0)

    quarter = half_rows // 4
    x = [z_ref[pl.ds(step * half_rows + part * quarter, quarter), :] for part in range(4)]
    x = [x[0] + x[2], x[1] + x[3], x[0] - x[2], x[1] - x[3]]
    for q, value in enumerate(exchanged(x, [pltpu.roll(i, 64, 1) for i in x])):
        x_ref[pl.ds(q, quarter, stride=4), :] = weights_ref[q] * value
    paired = x_ref[...].astype(BF)
    folded = lax.dot_general(paired, leg_ref[0], (((0,), (0,)), ((), ())), preferred_element_type=F32)
    half = folded.shape[0] // 2
    keep, even = kept(first_ref[0] + step, (half, folded.shape[1]), half // 2)
    chosen = jnp.where(even, folded[:half], folded[half:])
    out_ref[0] = jnp.where(keep, chosen, 0.0).astype(BF)


def legendre_call(kernel, name, extra, first, operands, in_specs, out_spec, out_shape, geometry, legendre):
    m_count, half_rows, k_count = legendre.shape
    levs = geometry[1]
    return pl.pallas_call(
        functools.partial(kernel, geometry),
        grid=(m_count,),
        in_specs=[pl.BlockSpec(memory_space=pltpu.SMEM)]
        + in_specs
        + [pl.BlockSpec((1, half_rows, k_count), lambda m: (m, 0, 0))],
        out_specs=out_spec,
        out_shape=out_shape,
        scratch_shapes=[
            pltpu.VMEM((m_count * half_rows, LANES), F32),
            pltpu.VMEM((levs, PIECE_ROWS, LANES), F32),
        ]
        + [pltpu.VMEM((half_rows, LANES), F32)] * extra,
        cost_estimate=pl.CostEstimate(
            flops=2 * legendre.size * LANES, bytes_accessed=2 * legendre.size + 5 * 10**6, transcendentals=0
        ),
        name=name,
    )(first.reshape(1), *operands, legendre)


PARTS = 4


def grid_kernel(owners, steps, table_ref, values_ref, out_ref, pack_ref):
    step = pl.program_id(0)
    groups = values_ref.shape[0] // LANES
    rows = out_ref.shape[1]
    result = lax.dot_general(table_ref[...], values_ref[...], (((1,), (1,)), ((), ())), preferred_element_type=F32)
    for part in range(PARTS):
        for g in range(groups):
            start = g * (PARTS * steps) + step * PARTS + part
            pack_ref[pl.ds(start, owners, stride=rows), :] = result[
                part * owners : (part + 1) * owners, g * LANES : (g + 1) * LANES
            ]

    @pl.when(step == steps - 1)
    def _():
        blank = jnp.zeros((owners, LANES), F32)
        for row in range(groups * (table_ref.shape[0] // owners) * steps, rows):
            pack_ref[pl.ds(row, owners, stride=rows), :] = blank
        out_ref[...] = pack_ref[...].reshape(out_ref.shape).astype(BF)


def grid_to_pieces(table, values, owners):
    rows = table.shape[0] // owners
    block = PARTS * owners
    return pl.pallas_call(
        functools.partial(grid_kernel, owners, rows // PARTS),
        grid=(rows // PARTS,),
        in_specs=[
            pl.BlockSpec((block, NLON), lambda i: (i, 0)),
            pl.BlockSpec(values.shape, lambda i: (0, 0)),
        ],
        out_specs=pl.BlockSpec((owners, PIECE_ROWS, LANES), lambda i: (0, 0, 0)),
        out_shape=jax.ShapeDtypeStruct((owners, PIECE_ROWS, LANES), BF),
        scratch_shapes=[pltpu.VMEM((owners * PIECE_ROWS, LANES), F32)],
        cost_estimate=pl.CostEstimate(
            flops=2 * table.size * values.shape[0], bytes_accessed=2 * table.size + 5 * 10**6, transcendentals=0
        ),
        name="grid_to_pieces",
    )(table, values)


def lane_ids(shape):
    return lax.broadcasted_iota(jnp.int32, shape, len(shape) - 1)


def edge_columns_kernel(tr_ref, head_ref, tail_ref, pad):
    rows, count, cols = tr_ref.shape[1:]
    lanes = lane_ids((count, LANES))
    head = jnp.zeros((count, LANES), F32)
    tail = head
    pad[:, :, :cols] = tr_ref[0]
    for r in range(rows):
        line = pad[r]
        here = (lanes >> 1) == r
        head = jnp.where(here, pltpu.roll(line, 2 * r, 1), head)
        tail = jnp.where(here, pltpu.roll(line, (2 * r - cols + 2) % LANES, 1), tail)
    head_ref[0] = head
    tail_ref[0] = tail


def with_columns(line, r, west, east, cols, lanes):
    line = jnp.where((lanes >> 1) == cols // 2, pltpu.roll(east, (cols - 2 * r) % LANES, 1), line)
    return jnp.where((lanes >> 1) == LANES // 2 - 1, pltpu.roll(west, (LANES - 2 - 2 * r) % LANES, 1), line)


def edge_rows_kernel(rows, first_ref, last_ref, west_ref, east_ref, top_ref, low_ref):
    count, cols = first_ref.shape[2:]
    lanes = lane_ids((count, LANES))
    west, east = west_ref[0], east_ref[0]
    for at in range(HALO):
        for src, out, r in ((first_ref, top_ref, at), (last_ref, low_ref, rows - HALO + at)):
            out[0, at, :, :cols] = src[0, at]
            out[0, at] = with_columns(out[0, at], r, west, east, cols, lanes)


def chemistry_kernel(
    total_rows, first_ref, tr_ref, north_ref, south_ref, west_ref, east_ref, u_ref, v_ref, react_ref, heat_ref,
    mix_ref, heating_ref, x_ref, y_ref, coef_ref,
):
    rows, tracers, cols = tr_ref.shape[1:]
    deep = rows + 2 * HALO
    lanes = lane_ids((tracers, LANES))
    west, east = west_ref[0], east_ref[0]
    for at in range(HALO):
        x_ref[at] = north_ref[0, at]
        x_ref[rows + HALO + at] = south_ref[0, at]
    x_ref[HALO : HALO + rows, :, :cols] = tr_ref[0]
    for r in range(rows):
        x_ref[HALO + r] = with_columns(x_ref[HALO + r], r, west, east, cols, lanes)
    u, v = u_ref[0], v_ref[0]
    face_u = 0.5 * (u + pltpu.roll(u, LANES - 1, 1))
    east_up, east_down = COURANT * jnp.maximum(face_u, 0.0), COURANT * jnp.minimum(face_u, 0.0)
    face_v = 0.5 * (v + pltpu.roll(v, deep - 1, 0))
    row = first_ref[0] - HALO + lax.broadcasted_iota(jnp.int32, face_v.shape, 0)
    face_v = jnp.where((row >= 0) & (row + 1 <= total_rows - 1), face_v, 0.0)
    south_up, south_down = COURANT * jnp.maximum(face_v, 0.0), COURANT * jnp.minimum(face_v, 0.0)
    coef_ref[0] = 1.0 - east_up + pltpu.roll(east_down, 1, 1) - south_up + pltpu.roll(south_down, 1, 0)
    coef_ref[1] = -east_down
    coef_ref[2] = pltpu.roll(east_up, 1, 1)
    coef_ref[3] = -south_down
    coef_ref[4] = pltpu.roll(south_up, 1, 0)
    react = react_ref[...]

    def moved(src, r):
        q = src[r]
        return (
            coef_ref[0, r : r + 1] * q
            + coef_ref[1, r : r + 1] * pltpu.roll(q, LANES - 1, 1)
            + coef_ref[2, r : r + 1] * pltpu.roll(q, 1, 1)
            + coef_ref[3, r : r + 1] * src[r + 1]
            + coef_ref[4, r : r + 1] * src[r - 1]
        )

    def step(src, r):
        both = jnp.concatenate([moved(src, r), moved(src, r + 1)], axis=1)
        high = both.astype(BF)
        low = (both - high.astype(F32)).astype(BF)
        return both + jnp.dot(react, jnp.concatenate([high, high, low], axis=0), preferred_element_type=F32)

    for r in range(1, deep - 1, 2):
        both = step(x_ref, r)
        y_ref[r] = both[:, :LANES]
        y_ref[r + 1] = both[:, LANES:]
    heat = heat_ref[...]
    heating_ref[0] = jnp.zeros_like(heating_ref[0])
    for r in range(HALO, rows + HALO, 2):
        both = step(y_ref, r)
        for at in range(2):
            one = both[:, at * LANES : (at + 1) * LANES]
            mix_ref[0, r - HALO + at] = one[:, :cols]
            warm = jnp.sum(heat * one, axis=0, keepdims=True)
            heating_ref[0, r + at : r + at + 1] = jnp.where(lanes[:1] < cols, warm, 0.0)


def shift(value, axis, by):
    count = lax.axis_size(axis)
    return lax.ppermute(value, axis, [(i, (i + by) % count) for i in range(count)])


def tracer_halos(tracers):
    levels, rows, count, cols = tracers.shape
    tr_spec = pl.BlockSpec((1, rows, count, cols), lambda l: (l, 0, 0, 0))
    col_spec = pl.BlockSpec((1, count, LANES), lambda l: (l, 0, 0))
    row_spec = pl.BlockSpec((1, HALO, count, LANES), lambda l: (l, 0, 0, 0))
    col_shape = jax.ShapeDtypeStruct((levels, count, LANES), F32)
    row_shape = jax.ShapeDtypeStruct((levels, HALO, count, LANES), F32)
    head, tail = pl.pallas_call(
        edge_columns_kernel,
        grid=(levels,),
        in_specs=[tr_spec],
        out_specs=[col_spec] * 2,
        out_shape=[col_shape] * 2,
        scratch_shapes=[pltpu.VMEM((rows, count, LANES), F32)],
        cost_estimate=pl.CostEstimate(flops=10**7, bytes_accessed=7 * 10**6, transcendentals=0),
        name="edge_columns",
    )(tracers)
    west = shift(tail, "lev", 1)
    east = shift(head, "lev", -1)
    top, low = pl.pallas_call(
        functools.partial(edge_rows_kernel, rows),
        grid=(levels,),
        in_specs=[
            pl.BlockSpec((1, HALO, count, cols), lambda l: (l, 0, 0, 0)),
            pl.BlockSpec((1, HALO, count, cols), lambda l: (l, rows // HALO - 1, 0, 0)),
            col_spec,
            col_spec,
        ],
        out_specs=[row_spec] * 2,
        out_shape=[row_shape] * 2,
        cost_estimate=pl.CostEstimate(flops=10**6, bytes_accessed=2 * 10**6, transcendentals=0),
        name="edge_rows",
    )(tracers, tracers, west, east)
    return shift(low, "wave", 1), shift(top, "wave", -1), west, east


def chemistry(tracers, halos, winds, reaction, heat_coeff, row_first, total_rows):
    levels, rows, count, cols = tracers.shape
    deep = rows + 2 * HALO
    high = reaction.astype(BF)
    low = (reaction - high.astype(F32)).astype(BF)
    react = jnp.concatenate([high, low, high], axis=1)
    heat = jnp.broadcast_to(heat_coeff[:, None], (count, LANES))
    tr_spec = pl.BlockSpec((1, rows, count, cols), lambda l: (l, 0, 0, 0))
    col_spec = pl.BlockSpec((1, count, LANES), lambda l: (l, 0, 0))
    row_spec = pl.BlockSpec((1, HALO, count, LANES), lambda l: (l, 0, 0, 0))
    whole = lambda shape: pl.BlockSpec(shape, lambda l: (0,) * len(shape))
    return pl.pallas_call(
        functools.partial(chemistry_kernel, total_rows),
        grid=(levels,),
        in_specs=[
            pl.BlockSpec(memory_space=pltpu.SMEM),
            tr_spec,
            row_spec,
            row_spec,
            col_spec,
            col_spec,
            pl.BlockSpec((1, deep, LANES), lambda l: (l, 0, 0)),
            pl.BlockSpec((1, deep, LANES), lambda l: (l + levels, 0, 0)),
            whole(react.shape),
            whole(heat.shape),
        ],
        out_specs=[tr_spec, pl.BlockSpec((1, deep, LANES), lambda l: (l, 0, 0))],
        out_shape=[
            jax.ShapeDtypeStruct(tracers.shape, F32),
            jax.ShapeDtypeStruct((levels, deep, LANES), F32),
        ],
        scratch_shapes=[
            pltpu.VMEM((deep, count, LANES), F32),
            pltpu.VMEM((deep, count, LANES), F32),
            pltpu.VMEM((5, deep, LANES), F32),
        ],
        cost_estimate=pl.CostEstimate(flops=10**9, bytes_accessed=16 * 10**6, transcendentals=0),
        name="chemistry",
    )(row_first.reshape(1), tracers, *halos, winds, winds, react, heat)


def body(spectra, legendre, gauss_weights, phys_matrix, phys_bias, tracers, reaction, heat_coeff):
    waves = lax.axis_size("wave")
    levs = lax.axis_size("lev")
    both = ("wave", "lev")
    wave, lev = lax.axis_index("wave"), lax.axis_index("lev")
    m_count, k_count, _, fields = spectra.shape
    half_rows = legendre.shape[1]
    levels, _, chem_rows, chem_cols = tracers.shape
    ratio = NLON // (chem_cols * levs)
    bands = waves // 2
    groups = (chem_rows + 2 * HALO) // levs
    south = wave >= bands
    width = 2 * fields

    owners = waves * levs
    geometry = (waves, levs, groups, bands, chem_rows, m_count)
    first_m = (wave * levs + lev) * m_count
    piece_shape = (owners, PIECE_ROWS, LANES)
    piece_spec = pl.BlockSpec(piece_shape, lambda m: (0, 0, 0))
    spec_spec = pl.BlockSpec((1, width, k_count), lambda m: (m, 0, 0))
    used = groups * 2 * m_count
    tracers = tracers.transpose(0, 2, 1, 3)

    pieces = legendre_call(
        inverse_kernel,
        "to_latitude",
        2,
        first_m,
        [spectra.transpose(0, 2, 3, 1).reshape(m_count, width, k_count)],
        [spec_spec],
        piece_spec,
        jax.ShapeDtypeStruct(piece_shape, BF),
        geometry,
        legendre,
    )
    spread = lax.all_to_all(pieces, both, split_axis=0, concat_axis=0, tiled=True)
    halos = tracer_halos(tracers)
    inverse, direct = fourier_tables(owners, m_count)
    spread = spread[:, :used].transpose(1, 0, 2).reshape(groups, 2 * TRUNC, LANES)

    grid = jnp.einsum("gkn,kj->gnj", spread, inverse, preferred_element_type=F32).astype(BF)
    grid = grid.reshape(groups, ratio, fields, NLON)

    lane = jnp.arange(LANES, dtype=jnp.int32)
    column = jnp.where(lane < LANES - HALO, lane, lane - LANES)
    column = (column[None, :] + chem_cols * jnp.arange(levs, dtype=jnp.int32)[:, None]) % (chem_cols * levs)
    held = (lane < chem_cols + HALO) | (lane >= LANES - HALO)
    column = jnp.where(held[None, :], column, -1).reshape(levs * LANES)
    cell = jnp.arange(NLON, dtype=jnp.int32) // ratio
    mean = jnp.where(cell[:, None] == column[None, :], 1.0 / ratio**2, 0.0).astype(BF)
    winds = jnp.einsum("gqfj,jx->gfx", grid[:, :, : 2 * levels], mean, preferred_element_type=F32)
    winds = winds.reshape(groups * 2 * levels, levs, LANES).transpose(1, 0, 2)
    winds = lax.all_to_all(winds, "lev", split_axis=0, concat_axis=0, tiled=True)
    winds = winds.reshape(levs * groups, 2 * levels, LANES)
    winds = jnp.where(south, jnp.flip(winds, axis=0), winds).transpose(1, 0, 2)

    mixing, heating = chemistry(
        tracers, halos, winds, reaction, heat_coeff, wave * chem_rows, chem_rows * waves
    )
    heating = heating.transpose(1, 0, 2)
    heating = jnp.where(south, jnp.flip(heating, axis=0), heating).reshape(levs, groups * levels, LANES)
    heating = lax.all_to_all(heating, "lev", split_axis=0, concat_axis=0, tiled=True)
    heating = heating.transpose(1, 0, 2).reshape(groups * levels, levs * LANES)
    high = heating.astype(BF)
    low = (heating - high.astype(F32)).astype(BF)
    column = jnp.where(lane[None, :] < chem_cols, lane + chem_cols * jnp.arange(levs, dtype=jnp.int32)[:, None], -1)
    copied = (column.reshape(levs * LANES)[:, None] == cell[None, :]).astype(BF)
    heating = jnp.dot(jnp.concatenate([high, low]), copied, preferred_element_type=F32)
    heating = (heating[: groups * levels] + heating[groups * levels :]).reshape(groups, 1, levels, NLON)

    physics = jnp.tanh(
        jnp.einsum("ef,gqfj->gqej", phys_matrix, grid.astype(F32), precision=lax.Precision.HIGHEST)
        + phys_bias[:, None]
    )
    tendency = jnp.concatenate(
        [physics[:, :, : 2 * levels], physics[:, :, 2 * levels : 3 * levels] + heating, physics[:, :, 3 * levels :]],
        axis=2,
    ).astype(BF)

    tendency = tendency.reshape(groups * ratio * fields, NLON)
    coeffs = grid_to_pieces(direct, tendency, owners)
    values = lax.all_to_all(coeffs, both, split_axis=0, concat_axis=0, tiled=True)

    result = legendre_call(
        direct_kernel,
        "to_spectral",
        1,
        first_m,
        [values, jnp.broadcast_to(gauss_weights.reshape(-1, 4).T[:, :, None], (4, half_rows // 4, LANES))],
        [piece_spec, pl.BlockSpec((4, half_rows // 4, LANES), lambda m: (0, 0, 0))],
        spec_spec,
        jax.ShapeDtypeStruct((m_count, width, k_count), BF),
        geometry,
        legendre,
    )
    result = result.reshape(m_count, 2, fields, k_count).transpose(0, 3, 1, 2)
    mixing = mixing.transpose(0, 2, 1, 3)
    return (result, mixing)


def solution(mesh):
    return jax.shard_map(
        body,
        mesh=mesh,
        in_specs=(
            P(("wave", "lev"), None, None, None),
            P(("wave", "lev"), None, None),
            P(),
            P(),
            P(),
            P(None, None, "wave", "lev"),
            P(),
            P(),
        ),
        out_specs=(P(("wave", "lev"), None, None, None), P(None, None, "wave", "lev")),
        check_vma=False,
    )
```

```python
import functools
import math

import jax
import jax.numpy as jnp
from jax import lax
from jax.experimental import pallas as pl
from jax.experimental.pallas import tpu as pltpu
from jax.sharding import PartitionSpec as P

TRUNC = 1280
NLON = 2560
HALF = NLON // 2
SUBSTEPS = 2
COURANT = 0.6
LANES = 128
FOLD = HALF + LANES
PIECE_ROWS = 64
UNIT = 8
HALO = 2
BF, F32 = jnp.bfloat16, jnp.float32


def table_kernel(cos_ref, sin_ref, turned_cos_ref, turned_sin_ref, a_ref, b_ref, out_ref):
    step = pl.program_id(0)
    for block in range(FOLD // LANES):
        part = slice(block * LANES, (block + 1) * LANES)
        cos, sin = (turned_cos_ref, turned_sin_ref) if block % 2 else (cos_ref, sin_ref)
        out_ref[:, part] = (cos[...] * a_ref[0, :, part] - sin[...] * b_ref[0, :, part]).astype(BF)

    @pl.when(step == 0)
    def _():
        top = out_ref[:16, :].astype(F32)
        first = lax.broadcasted_iota(jnp.int32, top.shape, 0) == 0
        out_ref[:16, :] = jnp.where(first, 0.5 * top, top).astype(BF)


def fourier_table(owners, m_count):
    unit = 2.0 * math.pi / NLON
    owner = jnp.arange(owners, dtype=jnp.int32)[:, None]
    lane = jnp.arange(LANES, dtype=jnp.int32)[None, :]
    coarse = (m_count * owner * lane % NLON).astype(F32) * unit
    cos_c, sin_c = jnp.cos(coarse), jnp.sin(coarse)
    turn = jnp.where(owner % 2 == 1, -1.0, 1.0).astype(F32)
    inner = jnp.arange(m_count, dtype=jnp.int32)[:, None]
    fine = (inner * jnp.arange(FOLD, dtype=jnp.int32)[None, :] % NLON).astype(F32) * unit
    cos, sin = jnp.cos(fine), jnp.sin(fine)
    a = 2.0 * jnp.concatenate([cos, -sin])
    b = 2.0 * jnp.concatenate([sin, cos])
    rows = 2 * m_count
    coarse_spec = pl.BlockSpec((owners, LANES), lambda i: (0, 0))
    fine_spec = pl.BlockSpec((1, 1, FOLD), lambda i: (i, 0, 0))
    out_spec = pl.BlockSpec((owners, FOLD), lambda i: (i, 0))
    shape = jax.ShapeDtypeStruct((owners * rows, FOLD), BF)
    return pl.pallas_call(
        table_kernel,
        grid=(rows,),
        in_specs=[coarse_spec] * 4 + [fine_spec] * 2,
        out_specs=out_spec,
        out_shape=shape,
        cost_estimate=pl.CostEstimate(flops=6 * TRUNC * FOLD, bytes_accessed=4 * TRUNC * FOLD, transcendentals=0),
        name="fourier_table",
    )(cos_c, sin_c, turn * cos_c, turn * sin_c, a[:, None], b[:, None])


def exchanged(x, turned):
    lanes = lane_ids(x[0].shape)
    low, even = lanes < 64, (lanes & 32) == 0
    pairs = [(jnp.where(low, x[i], turned[i + 2]), jnp.where(low, turned[i], x[i + 2])) for i in range(2)]
    out = []
    for first, second in zip(*pairs):
        out.append(jnp.where(even, first, pltpu.roll(second, 32, 1)))
        out.append(jnp.where(even, pltpu.roll(first, LANES - 32, 1), second))
    return out


def kept(m, shape, part_rows):
    row = lax.broadcasted_iota(jnp.int32, shape, 0)
    k = lax.broadcasted_iota(jnp.int32, shape, 1)
    return (k < TRUNC - m) & ((row < part_rows) | (m > 0)), k % 2 == 0


def inverse_kernel(geometry, first_ref, spec_ref, leg_ref, out_ref, z_ref, q_ref, x_ref, turned_ref):
    waves, levs, groups, bands, band_groups, m_count = geometry
    half_rows = leg_ref.shape[1]
    step = pl.program_id(0)
    spec = spec_ref[0].astype(F32)
    keep, even = kept(first_ref[0] + step, spec.shape, spec.shape[0] // 2)
    spec = jnp.where(keep, spec, 0.0)
    other = jnp.where(even, spec, -spec)
    stacked = jnp.concatenate([spec, other, other, spec], axis=0).astype(BF)
    values = lax.dot_general(leg_ref[0], stacked, (((1,), (1,)), ((), ())), preferred_element_type=F32)
    x_ref[...] = values[:, :LANES]
    turned_ref[...] = values[:, LANES:]
    quarter = half_rows // 4
    lines = [pl.ds(q, quarter, stride=4) for q in range(4)]
    for part, value in enumerate(exchanged([x_ref[i, :] for i in lines], [turned_ref[i, :] for i in lines])):
        z_ref[pl.ds(step * half_rows + part * quarter, quarter), :] = value

    @pl.when(step == m_count - 1)
    def _():
        q_ref[...] = jnp.zeros_like(q_ref)

        def of_wave(wave, carry):
            south = (wave >= bands).astype(jnp.int32)
            band = jnp.where(wave >= bands, waves - 1 - wave, wave)
            for lev in range(levs):
                for g in range(groups):
                    slot = lev * groups + g
                    at = band * band_groups + jnp.where(south == 1, band_groups + HALO - 1 - slot, slot - HALO)
                    over = at >= bands * band_groups
                    line = jnp.where(over, 2 * bands * band_groups - 1 - at, jnp.maximum(at, 0))
                    base = line + jnp.where(over, 1 - south, south) * (half_rows // 2)
                    for c in range(2):
                        for row, count, skip in moves(geometry, half_rows, slot, c):
                            start = base + (c * (half_rows // 4) + skip)
                            q_ref[lev, row : row + count] = z_ref[pl.ds(start, count, stride=half_rows), :]
                out_ref[wave * levs + lev] = q_ref[lev].astype(BF)
            return carry

        lax.fori_loop(0, waves, of_wave, 0)


def direct_kernel(geometry, first_ref, values_ref, weights_ref, leg_ref, out_ref, z_ref, q_ref, x_ref, w_ref):
    waves, levs, groups, bands, band_groups, m_count = geometry
    half_rows = leg_ref.shape[1]
    step = pl.program_id(0)

    @pl.when(step == 0)
    def _():
        for q in range(4):
            rows = pl.ds(q * (half_rows // 4), half_rows // 4)
            w_ref[rows, :] = jnp.broadcast_to(weights_ref[:, q : q + 1], (half_rows // 4, LANES))

        def of_wave(wave, carry):
            south = (wave >= bands).astype(jnp.int32)
            band = jnp.where(wave >= bands, waves - 1 - wave, wave)
            for lev in range(levs):
                q_ref[lev] = values_ref[wave * levs + lev].astype(F32)
                for g in range(groups):
                    slot = lev * groups + g
                    if HALO <= slot < band_groups + HALO:
                        inside = jnp.where(south == 1, band_groups + HALO - 1 - slot, slot - HALO)
                        base = band * band_groups + inside + south * (half_rows // 2)
                        for c in range(2):
                            for row, count, skip in moves(geometry, half_rows, slot, c):
                                start = base + (c * (half_rows // 4) + skip)
                                z_ref[pl.ds(start, count, stride=half_rows), :] = q_ref[lev, row : row + count]
            return carry

        lax.fori_loop(0, waves, of_wave, 0)

    quarter = half_rows // 4
    x = [z_ref[pl.ds(step * half_rows + part * quarter, quarter), :] for part in range(4)]
    x = [x[0] + x[2], x[1] + x[3], x[0] - x[2], x[1] - x[3]]
    for q, value in enumerate(exchanged(x, [pltpu.roll(i, 64, 1) for i in x])):
        x_ref[pl.ds(q, quarter, stride=4), :] = w_ref[pl.ds(q * quarter, quarter), :] * value
    paired = x_ref[...].astype(BF)
    folded = lax.dot_general(paired, leg_ref[0], (((0,), (0,)), ((), ())), preferred_element_type=F32)
    half = folded.shape[0] // 2
    keep, even = kept(first_ref[0] + step, (half, folded.shape[1]), half // 2)
    chosen = jnp.where(even, folded[:half], folded[half:])
    out_ref[0] = jnp.where(keep, chosen, 0.0).astype(BF)


def moves(geometry, half_rows, slot, c):
    m_count = geometry[-1]
    units = 2 * geometry[2]
    unit = 2 * (slot % geometry[2]) + c
    tail = m_count - UNIT
    return (unit * UNIT, UNIT, 0), (units * UNIT + unit * tail, tail, UNIT * half_rows)


def legendre_call(kernel, name, extra, first, operands, in_specs, out_spec, out_shape, geometry, legendre):
    m_count, half_rows, k_count = legendre.shape
    levs = geometry[1]
    return pl.pallas_call(
        functools.partial(kernel, geometry),
        grid=(m_count,),
        in_specs=[pl.BlockSpec(memory_space=pltpu.SMEM)]
        + in_specs
        + [pl.BlockSpec((1, half_rows, k_count), lambda m: (m, 0, 0))],
        out_specs=out_spec,
        out_shape=out_shape,
        scratch_shapes=[
            pltpu.VMEM((m_count * half_rows, LANES), F32),
            pltpu.VMEM((levs, PIECE_ROWS, LANES), F32),
        ]
        + [pltpu.VMEM((half_rows, LANES), F32)] * extra,
        cost_estimate=pl.CostEstimate(
            flops=2 * legendre.size * LANES, bytes_accessed=2 * legendre.size + 5 * 10**6, transcendentals=0
        ),
        name=name,
    )(first.reshape(1), *operands, legendre)


PARTS = 5


def grid_kernel(owners, steps, table_ref, *refs):
    value_refs, warm_refs, (heat_ref, out_ref, pack_ref, fold_ref) = refs[:2], refs[2:4], refs[4:]
    step = pl.program_id(0)
    lines = value_refs[0].shape[0]
    groups = lines // LANES
    rows = out_ref.shape[1]
    m_count = steps * PARTS // 2

    @pl.when(step == 0)
    def _():
        scale = 0.5 / math.sqrt(NLON)
        start = lane_ids((lines, LANES)) == 0
        columns = lines // 32
        levels = warm_refs[0].shape[0] // columns
        below = heat_ref.shape[0] // 2

        def tendency(side, block):
            part = slice(block * LANES, (block + 1) * LANES)
            there = slice(side * HALF + block * LANES, side * HALF + (block + 1) * LANES)
            value = value_refs[side][:, part].astype(F32)
            pieces = []
            for at in range(columns):
                cell = at // (columns // groups) * levels
                heat = heat_ref[cell : cell + levels, there] + heat_ref[below + cell : below + cell + levels, there]
                warm = warm_refs[side][at * levels : (at + 1) * levels, part] + heat
                pieces += [value[at * 32 : at * 32 + 2 * levels], warm.astype(BF).astype(F32)]
                pieces += [value[at * 32 + 3 * levels : (at + 1) * 32]]
            return jnp.concatenate(pieces, axis=0)

        for block in range(HALF // LANES):
            west, east = tendency(0, block), tendency(1, block)
            total = west + east
            if block == 0:
                total = jnp.where(start, west, total)
                fold_ref[0, :, HALF:] = jnp.where(start, scale * east, 0.0).astype(BF)
                fold_ref[1, :, HALF:] = jnp.zeros((lines, LANES), BF)
            fold_ref[0, :, block * LANES : (block + 1) * LANES] = (scale * total).astype(BF)
            fold_ref[1, :, block * LANES : (block + 1) * LANES] = (scale * (west - east)).astype(BF)

    part_c = step // (steps // 2)
    result = lax.dot_general(
        table_ref[...], fold_ref[part_c], (((1,), (1,)), ((), ())), preferred_element_type=F32
    )
    first = (lax.broadcasted_iota(jnp.int32, (owners, LANES), 0) == 0) & (step == 0)
    tail = m_count - UNIT
    for part in range(PARTS):
        m = step % (steps // 2) * PARTS + part
        for g in range(groups):
            unit = 2 * g + part_c
            start = jnp.where(m < UNIT, unit * UNIT + m, 2 * groups * UNIT + unit * tail + m - UNIT)
            value = result[part * owners : (part + 1) * owners, g * LANES : (g + 1) * LANES]
            if part == 0:
                value = jnp.where(first, 2.0 * value, value)
            pack_ref[pl.ds(start, owners, stride=rows), :] = value

    @pl.when(step == steps - 1)
    def _():
        blank = jnp.zeros((owners, LANES), F32)
        for row in range(groups * PARTS * steps, rows):
            pack_ref[pl.ds(row, owners, stride=rows), :] = blank
        out_ref[...] = pack_ref[...].reshape(out_ref.shape).astype(BF)


def grid_to_pieces(table, values, warm, heating, owners):
    steps = table.shape[0] // owners // PARTS
    return pl.pallas_call(
        functools.partial(grid_kernel, owners, steps),
        grid=(steps,),
        in_specs=[
            pl.BlockSpec((PARTS * owners, FOLD), lambda i: (i, 0)),
            *[pl.BlockSpec(value.shape, lambda i: (0, 0)) for value in (*values, *warm, heating)],
        ],
        out_specs=pl.BlockSpec((owners, PIECE_ROWS, LANES), lambda i: (0, 0, 0)),
        out_shape=jax.ShapeDtypeStruct((owners, PIECE_ROWS, LANES), BF),
        scratch_shapes=[
            pltpu.VMEM((owners * PIECE_ROWS, LANES), F32),
            pltpu.VMEM((2, values[0].shape[0], FOLD), BF),
        ],
        cost_estimate=pl.CostEstimate(
            flops=2 * table.size * values[0].shape[0], bytes_accessed=2 * table.size + 5 * 10**6, transcendentals=0
        ),
        name="grid_to_pieces",
    )(table, *values, *warm, heating)


def lane_ids(shape):
    return lax.broadcasted_iota(jnp.int32, shape, len(shape) - 1)


def edge_columns_kernel(tr_ref, head_ref, tail_ref, pad):
    rows, count, cols = tr_ref.shape[1:]
    lanes = lane_ids((count, LANES))
    head = jnp.zeros((count, LANES), F32)
    tail = head
    pad[:, :, :cols] = tr_ref[0]
    gap = LANES - HALO - cols
    for r in range(rows):
        line = pad[r]
        head = jnp.where((lanes >> 1) == r, pltpu.roll(line, 2 * r, 1), head)
        tail = jnp.where((lanes >> 1) == r + gap // 2, pltpu.roll(line, (2 * r + gap - cols + HALO) % LANES, 1), tail)
    head_ref[0] = head.astype(BF)
    tail_ref[0] = tail.astype(BF)


def both_sides(west, east, cols, lanes):
    return jnp.where(lanes < LANES - HALO - cols, east.astype(F32), west.astype(F32))


def with_columns(line, r, sides, cols, lanes):
    here = ((lanes >> 1) == cols // 2) | ((lanes >> 1) == LANES // 2 - 1)
    return jnp.where(here, pltpu.roll(sides, (cols - 2 * r) % LANES, 1), line)


def edge_rows_kernel(rows, first_ref, last_ref, west_ref, east_ref, top_ref, low_ref, line):
    levels, _, count, cols = first_ref.shape
    lanes = lane_ids((count, LANES))
    for level in range(levels):
        sides = both_sides(west_ref[level], east_ref[level], cols, lanes)
        for at in range(HALO):
            for src, out, r in ((first_ref, top_ref, at), (last_ref, low_ref, rows - HALO + at)):
                line[:, :cols] = src[level, at]
                out[level, at] = with_columns(line[...], r, sides, cols, lanes).astype(BF)


def chemistry_kernel(
    total_rows, first_ref, tr_ref, north_ref, south_ref, west_ref, east_ref, u_ref, v_ref, react_ref, heat_ref,
    mix_ref, heating_ref, x_ref, y_ref, coef_ref,
):
    rows, tracers, cols = tr_ref.shape[1:]
    deep = rows + 2 * HALO
    lanes = lane_ids((tracers, LANES))
    sides = both_sides(west_ref[0], east_ref[0], cols, lanes)
    for at in range(HALO):
        x_ref[at] = north_ref[0, at].astype(F32)
        x_ref[rows + HALO + at] = south_ref[0, at].astype(F32)
    x_ref[HALO : HALO + rows, :, :cols] = tr_ref[0]
    for r in range(rows):
        x_ref[HALO + r] = with_columns(x_ref[HALO + r], r, sides, cols, lanes)
    u, v = u_ref[0], v_ref[0]
    face_u = 0.5 * (u + pltpu.roll(u, LANES - 1, 1))
    east_up, east_down = COURANT * jnp.maximum(face_u, 0.0), COURANT * jnp.minimum(face_u, 0.0)
    face_v = 0.5 * (v + pltpu.roll(v, deep - 1, 0))
    row = first_ref[0] - HALO + lax.broadcasted_iota(jnp.int32, face_v.shape, 0)
    face_v = jnp.where((row >= 0) & (row + 1 <= total_rows - 1), face_v, 0.0)
    south_up, south_down = COURANT * jnp.maximum(face_v, 0.0), COURANT * jnp.minimum(face_v, 0.0)
    coef_ref[0] = 1.0 - east_up + pltpu.roll(east_down, 1, 1) - south_up + pltpu.roll(south_down, 1, 0)
    coef_ref[1] = -east_down
    coef_ref[2] = pltpu.roll(east_up, 1, 1)
    coef_ref[3] = -south_down
    coef_ref[4] = pltpu.roll(south_up, 1, 0)
    react = react_ref[...]

    def moved(src, r):
        q = src[r]
        return (
            coef_ref[0, r : r + 1] * q
            + coef_ref[1, r : r + 1] * pltpu.roll(q, LANES - 1, 1)
            + coef_ref[2, r : r + 1] * pltpu.roll(q, 1, 1)
            + coef_ref[3, r : r + 1] * src[r + 1]
            + coef_ref[4, r : r + 1] * src[r - 1]
        )

    def step(src, r):
        both = jnp.concatenate([moved(src, r), moved(src, r + 1)], axis=1)
        high = both.astype(BF)
        low = (both - high.astype(F32)).astype(BF)
        return both + jnp.dot(react, jnp.concatenate([high, high, low], axis=0), preferred_element_type=F32)

    for r in range(1, deep - 1, 2):
        both = step(x_ref, r)
        y_ref[r] = both[:, :LANES]
        y_ref[r + 1] = both[:, LANES:]
    heat = heat_ref[...]
    heating_ref[0] = jnp.zeros_like(heating_ref[0])
    for r in range(HALO, rows + HALO, 2):
        both = step(y_ref, r)
        for at in range(2):
            one = both[:, at * LANES : (at + 1) * LANES]
            mix_ref[0, r - HALO + at] = one[:, :cols]
            warm = jnp.sum(heat * one, axis=0, keepdims=True)
            heating_ref[0, r + at : r + at + 1] = jnp.where(lanes[:1] < cols, warm, 0.0)


def shift(value, axis, by):
    count = lax.axis_size(axis)
    return lax.ppermute(value, axis, [(i, (i + by) % count) for i in range(count)])


def tracer_halos(tracers):
    levels, rows, count, cols = tracers.shape
    tr_spec = pl.BlockSpec((1, rows, count, cols), lambda l: (l, 0, 0, 0))
    col_spec = pl.BlockSpec((1, count, LANES), lambda l: (l, 0, 0))
    col_shape = jax.ShapeDtypeStruct((levels, count, LANES), BF)
    row_shape = jax.ShapeDtypeStruct((levels, HALO, count, LANES), BF)
    some = levels // 2
    head, tail = pl.pallas_call(
        edge_columns_kernel,
        grid=(levels,),
        in_specs=[tr_spec],
        out_specs=[col_spec] * 2,
        out_shape=[col_shape] * 2,
        scratch_shapes=[pltpu.VMEM((rows, count, LANES), F32)],
        cost_estimate=pl.CostEstimate(flops=10**7, bytes_accessed=7 * 10**6, transcendentals=0),
        name="edge_columns",
    )(tracers)
    west = shift(tail, "lev", 1)
    east = shift(head, "lev", -1)
    top, low = pl.pallas_call(
        functools.partial(edge_rows_kernel, rows),
        grid=(levels // some,),
        in_specs=[
            pl.BlockSpec((some, HALO, count, cols), lambda l: (l, 0, 0, 0)),
            pl.BlockSpec((some, HALO, count, cols), lambda l: (l, rows // HALO - 1, 0, 0)),
            pl.BlockSpec((some, count, LANES), lambda l: (l, 0, 0)),
            pl.BlockSpec((some, count, LANES), lambda l: (l, 0, 0)),
        ],
        out_specs=[pl.BlockSpec((some, HALO, count, LANES), lambda l: (l, 0, 0, 0))] * 2,
        scratch_shapes=[pltpu.VMEM((count, LANES), F32)],
        out_shape=[row_shape] * 2,
        cost_estimate=pl.CostEstimate(flops=10**6, bytes_accessed=2 * 10**6, transcendentals=0),
        name="edge_rows",
    )(tracers, tracers, west, east)
    return shift(low, "wave", 1), shift(top, "wave", -1), west, east


def chemistry(tracers, halos, winds, reaction, heat_coeff, row_first, total_rows):
    levels, rows, count, cols = tracers.shape
    deep = rows + 2 * HALO
    high = reaction.astype(BF)
    low = (reaction - high.astype(F32)).astype(BF)
    react = jnp.concatenate([high, low, high], axis=1)
    heat = jnp.broadcast_to(heat_coeff[:, None], (count, LANES))
    tr_spec = pl.BlockSpec((1, rows, count, cols), lambda l: (l, 0, 0, 0))
    col_spec = pl.BlockSpec((1, count, LANES), lambda l: (l, 0, 0))
    row_spec = pl.BlockSpec((1, HALO, count, LANES), lambda l: (l, 0, 0, 0))
    whole = lambda shape: pl.BlockSpec(shape, lambda l: (0,) * len(shape))
    return pl.pallas_call(
        functools.partial(chemistry_kernel, total_rows),
        grid=(levels,),
        in_specs=[
            pl.BlockSpec(memory_space=pltpu.SMEM),
            tr_spec,
            row_spec,
            row_spec,
            col_spec,
            col_spec,
            pl.BlockSpec((1, deep, LANES), lambda l: (l, 0, 0)),
            pl.BlockSpec((1, deep, LANES), lambda l: (l + levels, 0, 0)),
            whole(react.shape),
            whole(heat.shape),
        ],
        out_specs=[tr_spec, pl.BlockSpec((1, deep, LANES), lambda l: (l, 0, 0))],
        out_shape=[
            jax.ShapeDtypeStruct(tracers.shape, F32),
            jax.ShapeDtypeStruct((levels, deep, LANES), F32),
        ],
        scratch_shapes=[
            pltpu.VMEM((deep, count, LANES), F32),
            pltpu.VMEM((deep, count, LANES), F32),
            pltpu.VMEM((5, deep, LANES), F32),
        ],
        cost_estimate=pl.CostEstimate(flops=10**9, bytes_accessed=16 * 10**6, transcendentals=0),
        name="chemistry",
    )(row_first.reshape(1), tracers, *halos, winds, winds, react, heat)


def body(spectra, legendre, gauss_weights, phys_matrix, phys_bias, tracers, reaction, heat_coeff):
    waves = lax.axis_size("wave")
    levs = lax.axis_size("lev")
    both = ("wave", "lev")
    wave, lev = lax.axis_index("wave"), lax.axis_index("lev")
    m_count, k_count, _, fields = spectra.shape
    half_rows = legendre.shape[1]
    levels, _, chem_rows, chem_cols = tracers.shape
    ratio = NLON // (chem_cols * levs)
    bands = waves // 2
    groups = (chem_rows + 2 * HALO) // levs
    width = 2 * fields

    owners = waves * levs
    geometry = (waves, levs, groups, bands, chem_rows, m_count)
    first_m = (wave * levs + lev) * m_count
    piece_shape = (owners, PIECE_ROWS, LANES)
    piece_spec = pl.BlockSpec(piece_shape, lambda m: (0, 0, 0))
    spec_spec = pl.BlockSpec((1, width, k_count), lambda m: (m, 0, 0))
    used = groups * 2 * m_count
    tracers = tracers.transpose(0, 2, 1, 3)

    pieces = legendre_call(
        inverse_kernel,
        "to_latitude",
        2,
        first_m,
        [spectra.transpose(0, 2, 3, 1).reshape(m_count, width, k_count)],
        [spec_spec],
        piece_spec,
        jax.ShapeDtypeStruct(piece_shape, BF),
        geometry,
        legendre,
    )
    spread = lax.all_to_all(pieces, both, split_axis=0, concat_axis=0, tiled=True)
    halos = tracer_halos(tracers)
    table = fourier_table(owners, m_count)
    spread = spread[:, :used].transpose(1, 0, 2)
    tiles = groups * 2 * UNIT
    spread = jnp.concatenate(
        [spread[:tiles].reshape(groups, 2, UNIT, owners, LANES), spread[tiles:].reshape(groups, 2, -1, owners, LANES)],
        axis=2,
    ).reshape(groups, 2, TRUNC, LANES)

    sums = jnp.einsum("gckn,ckj->cgnj", spread, table.reshape(2, TRUNC, FOLD), preferred_element_type=F32)
    cosine, sine, turn = sums[0, ..., :HALF], sums[1, ..., :HALF], sums[0, ..., HALF : HALF + 1]
    turned = jnp.where(jnp.arange(HALF, dtype=jnp.int32) == 0, turn, cosine - sine)
    halves = [value.astype(BF).reshape(groups, ratio, fields, HALF) for value in (cosine + sine, turned)]

    lane = jnp.arange(LANES, dtype=jnp.int32)
    column = jnp.where(lane < LANES - HALO, lane, lane - LANES)
    column = (column[None, :] + chem_cols * jnp.arange(levs, dtype=jnp.int32)[:, None]) % (chem_cols * levs)
    held = (lane < chem_cols + HALO) | (lane >= LANES - HALO)
    column = jnp.where(held[None, :], column, -1).reshape(levs * LANES)
    order = jnp.arange(NLON, dtype=jnp.int32)
    cell = jnp.where(order <= HALF, order, NLON + HALF - order) // ratio
    mean = jnp.where(cell[:, None] == column[None, :], 1.0 / ratio**2, 0.0).astype(BF)
    winds = sum(
        jnp.einsum("gqfj,jx->gqfx", half[:, :, : 2 * levels], part, preferred_element_type=F32).sum(axis=1)
        for half, part in zip(halves, (mean[:HALF], mean[HALF:]))
    )
    winds = winds.reshape(groups * 2 * levels, levs, LANES).transpose(1, 0, 2)
    winds = lax.all_to_all(winds, "lev", split_axis=0, concat_axis=0, tiled=True)
    winds = winds.reshape(levs * groups, 2 * levels, LANES).transpose(1, 0, 2)

    mixing, heating = chemistry(
        tracers, halos, winds, reaction, heat_coeff, wave * chem_rows, chem_rows * waves
    )
    heating = heating.transpose(1, 0, 2).reshape(levs, groups * levels, LANES)
    heating = lax.all_to_all(heating, "lev", split_axis=0, concat_axis=0, tiled=True)
    heating = heating.transpose(1, 0, 2).reshape(groups * levels, levs * LANES)
    high = heating.astype(BF)
    low = (heating - high.astype(F32)).astype(BF)
    column = jnp.where(lane[None, :] < chem_cols, lane + chem_cols * jnp.arange(levs, dtype=jnp.int32)[:, None], -1)
    copied = (column.reshape(levs * LANES)[:, None] == cell[None, :]).astype(BF)
    heating = jnp.dot(jnp.concatenate([high, low]), copied, preferred_element_type=F32)

    values, warm = [], []
    for half in halves:
        physics = jnp.tanh(
            jnp.einsum("ef,gqfj->gqej", phys_matrix, half.astype(F32), precision=lax.Precision.HIGHEST)
            + phys_bias[:, None]
        )
        values.append(physics.astype(BF).reshape(groups * ratio * fields, HALF))
        warm.append(physics[:, :, 2 * levels : 3 * levels].reshape(groups * ratio * levels, HALF))

    coeffs = grid_to_pieces(table, values, warm, heating, owners)
    values = lax.all_to_all(coeffs, both, split_axis=0, concat_axis=0, tiled=True)

    result = legendre_call(
        direct_kernel,
        "to_spectral",
        2,
        first_m,
        [values, gauss_weights.reshape(half_rows // 4, 4)],
        [piece_spec, pl.BlockSpec((half_rows // 4, 4), lambda m: (0, 0))],
        spec_spec,
        jax.ShapeDtypeStruct((m_count, width, k_count), BF),
        geometry,
        legendre,
    )
    result = result.reshape(m_count, 2, fields, k_count).transpose(0, 3, 1, 2)
    mixing = mixing.transpose(0, 2, 1, 3)
    return (result, mixing)


def solution(mesh):
    return jax.shard_map(
        body,
        mesh=mesh,
        in_specs=(
            P(("wave", "lev"), None, None, None),
            P(("wave", "lev"), None, None),
            P(),
            P(),
            P(),
            P(None, None, "wave", "lev"),
            P(),
            P(),
        ),
        out_specs=(P(("wave", "lev"), None, None, None), P(None, None, "wave", "lev")),
        check_vma=False,
    )
```

```python
import functools
import math

import jax
import jax.numpy as jnp
from jax import lax
from jax.experimental import pallas as pl
from jax.experimental.pallas import tpu as pltpu
from jax.sharding import PartitionSpec as P

TRUNC = 1280
NLON = 2560
HALF = NLON // 2
SUBSTEPS = 2
COURANT = 0.6
LANES = 128
FOLD = HALF + LANES
PIECE_ROWS = 64
UNIT = 8
HALO = 2
BF, F32 = jnp.bfloat16, jnp.float32


def table_kernel(cos_ref, sin_ref, turned_cos_ref, turned_sin_ref, a_ref, b_ref, out_ref):
    step = pl.program_id(0)
    owners = cos_ref.shape[0]
    for row in range(a_ref.shape[0]):
        for block in range(FOLD // LANES):
            part = slice(block * LANES, (block + 1) * LANES)
            cos, sin = (turned_cos_ref, turned_sin_ref) if block % 2 else (cos_ref, sin_ref)
            value = cos[...] * a_ref[row, :, part] - sin[...] * b_ref[row, :, part]
            out_ref[row * owners : (row + 1) * owners, part] = value.astype(BF)

    @pl.when(step == 0)
    def _():
        top = out_ref[:16, :].astype(F32)
        first = lax.broadcasted_iota(jnp.int32, top.shape, 0) == 0
        out_ref[:16, :] = jnp.where(first, 0.5 * top, top).astype(BF)


def fourier_table(owners, m_count):
    unit = 2.0 * math.pi / NLON
    owner = jnp.arange(owners, dtype=jnp.int32)[:, None]
    lane = jnp.arange(LANES, dtype=jnp.int32)[None, :]
    coarse = (m_count * owner * lane % NLON).astype(F32) * unit
    cos_c, sin_c = jnp.cos(coarse), jnp.sin(coarse)
    turn = jnp.where(owner % 2 == 1, -1.0, 1.0).astype(F32)
    inner = jnp.arange(m_count, dtype=jnp.int32)[:, None]
    fine = (inner * jnp.arange(FOLD, dtype=jnp.int32)[None, :] % NLON).astype(F32) * unit
    cos, sin = jnp.cos(fine), jnp.sin(fine)
    a = 2.0 * jnp.concatenate([cos, -sin])
    b = 2.0 * jnp.concatenate([sin, cos])
    rows = 2 * m_count
    coarse_spec = pl.BlockSpec((owners, LANES), lambda i: (0, 0))
    fine_spec = pl.BlockSpec((PARTS, 1, FOLD), lambda i: (i, 0, 0))
    out_spec = pl.BlockSpec((PARTS * owners, FOLD), lambda i: (i, 0))
    shape = jax.ShapeDtypeStruct((owners * rows, FOLD), BF)
    return pl.pallas_call(
        table_kernel,
        grid=(rows // PARTS,),
        in_specs=[coarse_spec] * 4 + [fine_spec] * 2,
        out_specs=out_spec,
        out_shape=shape,
        cost_estimate=pl.CostEstimate(flops=6 * TRUNC * FOLD, bytes_accessed=4 * TRUNC * FOLD, transcendentals=0),
        name="fourier_table",
    )(cos_c, sin_c, turn * cos_c, turn * sin_c, a[:, None], b[:, None])


def exchanged(x, turned):
    lanes = lane_ids(x[0].shape)
    low, even = lanes < 64, (lanes & 32) == 0
    pairs = [(jnp.where(low, x[i], turned[i + 2]), jnp.where(low, turned[i], x[i + 2])) for i in range(2)]
    out = []
    for first, second in zip(*pairs):
        out.append(jnp.where(even, first, pltpu.roll(second, 32, 1)))
        out.append(jnp.where(even, pltpu.roll(first, LANES - 32, 1), second))
    return out


def kept(m, shape, part_rows):
    row = lax.broadcasted_iota(jnp.int32, shape, 0)
    k = lax.broadcasted_iota(jnp.int32, shape, 1)
    return (k < TRUNC - m) & ((row < part_rows) | (m > 0)), k % 2 == 0


def inverse_kernel(geometry, first_ref, spec_ref, leg_ref, out_ref, z_ref, q_ref, x_ref, turned_ref):
    waves, levs, groups, bands, band_groups, m_count = geometry
    half_rows = leg_ref.shape[1]
    step = pl.program_id(0)
    spec = spec_ref[0].astype(F32)
    keep, even = kept(first_ref[0] + step, spec.shape, spec.shape[0] // 2)
    spec = jnp.where(keep, spec, 0.0)
    other = jnp.where(even, spec, -spec)
    stacked = jnp.concatenate([spec, other, other, spec], axis=0).astype(BF)
    values = lax.dot_general(leg_ref[0], stacked, (((1,), (1,)), ((), ())), preferred_element_type=F32)
    x_ref[...] = values[:, :LANES]
    turned_ref[...] = values[:, LANES:]
    quarter = half_rows // 4
    lines = [pl.ds(q, quarter, stride=4) for q in range(4)]
    for part, value in enumerate(exchanged([x_ref[i, :] for i in lines], [turned_ref[i, :] for i in lines])):
        z_ref[pl.ds(step * half_rows + part * quarter, quarter), :] = value

    @pl.when(step == m_count - 1)
    def _():
        q_ref[...] = jnp.zeros_like(q_ref)

        def of_wave(wave, carry):
            south = (wave >= bands).astype(jnp.int32)
            band = jnp.where(wave >= bands, waves - 1 - wave, wave)
            for lev in range(levs):
                for g in range(groups):
                    slot = lev * groups + g
                    at = band * band_groups + jnp.where(south == 1, band_groups + HALO - 1 - slot, slot - HALO)
                    over = at >= bands * band_groups
                    line = jnp.where(over, 2 * bands * band_groups - 1 - at, jnp.maximum(at, 0))
                    base = line + jnp.where(over, 1 - south, south) * (half_rows // 2)
                    for c in range(2):
                        for row, count, skip in moves(geometry, half_rows, slot, c):
                            start = base + (c * (half_rows // 4) + skip)
                            q_ref[lev, row : row + count] = z_ref[pl.ds(start, count, stride=half_rows), :]
                out_ref[wave * levs + lev] = q_ref[lev].astype(BF)
            return carry

        lax.fori_loop(0, waves, of_wave, 0)


def direct_kernel(geometry, first_ref, values_ref, weights_ref, leg_ref, out_ref, z_ref, q_ref, x_ref, w_ref):
    waves, levs, groups, bands, band_groups, m_count = geometry
    half_rows = leg_ref.shape[1]
    step = pl.program_id(0)

    @pl.when(step == 0)
    def _():
        for q in range(4):
            rows = pl.ds(q * (half_rows // 4), half_rows // 4)
            w_ref[rows, :] = jnp.broadcast_to(weights_ref[:, q : q + 1], (half_rows // 4, LANES))

        def of_wave(wave, carry):
            south = (wave >= bands).astype(jnp.int32)
            band = jnp.where(wave >= bands, waves - 1 - wave, wave)
            for lev in range(levs):
                q_ref[lev] = values_ref[wave * levs + lev].astype(F32)
                for g in range(groups):
                    slot = lev * groups + g
                    if HALO <= slot < band_groups + HALO:
                        inside = jnp.where(south == 1, band_groups + HALO - 1 - slot, slot - HALO)
                        base = band * band_groups + inside + south * (half_rows // 2)
                        for c in range(2):
                            for row, count, skip in moves(geometry, half_rows, slot, c):
                                start = base + (c * (half_rows // 4) + skip)
                                z_ref[pl.ds(start, count, stride=half_rows), :] = q_ref[lev, row : row + count]
            return carry

        lax.fori_loop(0, waves, of_wave, 0)

    quarter = half_rows // 4
    x = [z_ref[pl.ds(step * half_rows + part * quarter, quarter), :] for part in range(4)]
    x = [x[0] + x[2], x[1] + x[3], x[0] - x[2], x[1] - x[3]]
    for q, value in enumerate(exchanged(x, [pltpu.roll(i, 64, 1) for i in x])):
        x_ref[pl.ds(q, quarter, stride=4), :] = w_ref[pl.ds(q * quarter, quarter), :] * value
    paired = x_ref[...].astype(BF)
    folded = lax.dot_general(paired, leg_ref[0], (((0,), (0,)), ((), ())), preferred_element_type=F32)
    half = folded.shape[0] // 2
    keep, even = kept(first_ref[0] + step, (half, folded.shape[1]), half // 2)
    chosen = jnp.where(even, folded[:half], folded[half:])
    out_ref[0] = jnp.where(keep, chosen, 0.0).astype(BF)


def moves(geometry, half_rows, slot, c):
    m_count = geometry[-1]
    units = 2 * geometry[2]
    unit = 2 * (slot % geometry[2]) + c
    tail = m_count - UNIT
    return (unit * UNIT, UNIT, 0), (units * UNIT + unit * tail, tail, UNIT * half_rows)


def legendre_call(kernel, name, extra, first, operands, in_specs, out_spec, out_shape, geometry, legendre):
    m_count, half_rows, k_count = legendre.shape
    levs = geometry[1]
    return pl.pallas_call(
        functools.partial(kernel, geometry),
        grid=(m_count,),
        in_specs=[pl.BlockSpec(memory_space=pltpu.SMEM)]
        + in_specs
        + [pl.BlockSpec((1, half_rows, k_count), lambda m: (m, 0, 0))],
        out_specs=out_spec,
        out_shape=out_shape,
        scratch_shapes=[
            pltpu.VMEM((m_count * half_rows, LANES), F32),
            pltpu.VMEM((levs, PIECE_ROWS, LANES), F32),
        ]
        + [pltpu.VMEM((half_rows, LANES), F32)] * extra,
        cost_estimate=pl.CostEstimate(
            flops=2 * legendre.size * LANES, bytes_accessed=2 * legendre.size + 5 * 10**6, transcendentals=0
        ),
        name=name,
    )(first.reshape(1), *operands, legendre)


PARTS = 5


def grid_kernel(owners, steps, table_ref, *refs):
    value_refs, warm_refs, (heat_ref, out_ref, pack_ref, fold_ref) = refs[:2], refs[2:4], refs[4:]
    step = pl.program_id(0)
    lines = value_refs[0].shape[0]
    groups = lines // LANES
    rows = out_ref.shape[1]
    m_count = steps * PARTS // 2

    @pl.when(step == 0)
    def _():
        scale = 0.5 / math.sqrt(NLON)
        start = lane_ids((lines, LANES)) == 0
        columns = lines // 32
        levels = warm_refs[0].shape[0] // columns
        below = heat_ref.shape[0] // 2

        def tendency(side, block):
            part = slice(block * LANES, (block + 1) * LANES)
            there = slice(side * HALF + block * LANES, side * HALF + (block + 1) * LANES)
            value = value_refs[side][:, part].astype(F32)
            pieces = []
            for at in range(columns):
                cell = at // (columns // groups) * levels
                heat = heat_ref[cell : cell + levels, there] + heat_ref[below + cell : below + cell + levels, there]
                warm = warm_refs[side][at * levels : (at + 1) * levels, part] + heat
                pieces += [value[at * 32 : at * 32 + 2 * levels], warm.astype(BF).astype(F32)]
                pieces += [value[at * 32 + 3 * levels : (at + 1) * 32]]
            return jnp.concatenate(pieces, axis=0)

        for block in range(HALF // LANES):
            west, east = tendency(0, block), tendency(1, block)
            total = west + east
            if block == 0:
                total = jnp.where(start, west, total)
                fold_ref[0, :, HALF:] = jnp.where(start, scale * east, 0.0).astype(BF)
                fold_ref[1, :, HALF:] = jnp.zeros((lines, LANES), BF)
            fold_ref[0, :, block * LANES : (block + 1) * LANES] = (scale * total).astype(BF)
            fold_ref[1, :, block * LANES : (block + 1) * LANES] = (scale * (west - east)).astype(BF)

    part_c = step // (steps // 2)
    result = lax.dot_general(
        table_ref[...], fold_ref[part_c], (((1,), (1,)), ((), ())), preferred_element_type=F32
    )
    first = (lax.broadcasted_iota(jnp.int32, (owners, LANES), 0) == 0) & (step == 0)
    tail = m_count - UNIT
    for part in range(PARTS):
        m = step % (steps // 2) * PARTS + part
        for g in range(groups):
            unit = 2 * g + part_c
            start = jnp.where(m < UNIT, unit * UNIT + m, 2 * groups * UNIT + unit * tail + m - UNIT)
            value = result[part * owners : (part + 1) * owners, g * LANES : (g + 1) * LANES]
            if part == 0:
                value = jnp.where(first, 2.0 * value, value)
            pack_ref[pl.ds(start, owners, stride=rows), :] = value

    @pl.when(step == steps - 1)
    def _():
        blank = jnp.zeros((owners, LANES), F32)
        for row in range(groups * PARTS * steps, rows):
            pack_ref[pl.ds(row, owners, stride=rows), :] = blank
        out_ref[...] = pack_ref[...].reshape(out_ref.shape).astype(BF)


def grid_to_pieces(table, values, warm, heating, owners):
    steps = table.shape[0] // owners // PARTS
    return pl.pallas_call(
        functools.partial(grid_kernel, owners, steps),
        grid=(steps,),
        in_specs=[
            pl.BlockSpec((PARTS * owners, FOLD), lambda i: (i, 0)),
            *[pl.BlockSpec(value.shape, lambda i: (0, 0)) for value in (*values, *warm, heating)],
        ],
        out_specs=pl.BlockSpec((owners, PIECE_ROWS, LANES), lambda i: (0, 0, 0)),
        out_shape=jax.ShapeDtypeStruct((owners, PIECE_ROWS, LANES), BF),
        scratch_shapes=[
            pltpu.VMEM((owners * PIECE_ROWS, LANES), F32),
            pltpu.VMEM((2, values[0].shape[0], FOLD), BF),
        ],
        cost_estimate=pl.CostEstimate(
            flops=2 * table.size * values[0].shape[0], bytes_accessed=2 * table.size + 5 * 10**6, transcendentals=0
        ),
        name="grid_to_pieces",
    )(table, *values, *warm, heating)


def lane_ids(shape):
    return lax.broadcasted_iota(jnp.int32, shape, len(shape) - 1)


def edge_columns_kernel(tr_ref, head_ref, tail_ref, pad):
    levels, rows, count, cols = tr_ref.shape
    lanes = lane_ids((count, LANES))
    gap = LANES - HALO - cols
    for level in range(levels):
        head = jnp.zeros((count, LANES), F32)
        tail = head
        pad[level, :, :, :cols] = tr_ref[level]
        for r in range(rows):
            line = pad[level, r]
            head = jnp.where((lanes >> 1) == r, pltpu.roll(line, 2 * r, 1), head)
            tail = jnp.where(
                (lanes >> 1) == r + gap // 2, pltpu.roll(line, (2 * r + gap - cols + HALO) % LANES, 1), tail
            )
        head_ref[level] = head.astype(BF)
        tail_ref[level] = tail.astype(BF)


def both_sides(west, east, cols, lanes):
    return jnp.where(lanes < LANES - HALO - cols, east.astype(F32), west.astype(F32))


def with_columns(line, r, sides, cols, lanes):
    here = ((lanes >> 1) == cols // 2) | ((lanes >> 1) == LANES // 2 - 1)
    return jnp.where(here, pltpu.roll(sides, (cols - 2 * r) % LANES, 1), line)


def edge_rows_kernel(rows, first_ref, last_ref, west_ref, east_ref, top_ref, low_ref, line):
    levels, _, count, cols = first_ref.shape
    lanes = lane_ids((count, LANES))
    for level in range(levels):
        sides = both_sides(west_ref[level], east_ref[level], cols, lanes)
        for at in range(HALO):
            for src, out, r in ((first_ref, top_ref, at), (last_ref, low_ref, rows - HALO + at)):
                line[:, :cols] = src[level, at]
                out[level, at] = with_columns(line[...], r, sides, cols, lanes).astype(BF)


def chemistry_kernel(
    total_rows, first_ref, tr_ref, north_ref, south_ref, west_ref, east_ref, u_ref, v_ref, react_ref, heat_ref,
    mix_ref, heating_ref, x_ref, y_ref, coef_ref,
):
    rows, tracers, cols = tr_ref.shape[1:]
    deep = rows + 2 * HALO
    lanes = lane_ids((tracers, LANES))
    sides = both_sides(west_ref[0], east_ref[0], cols, lanes)
    for at in range(HALO):
        x_ref[at] = north_ref[0, at].astype(F32)
        x_ref[rows + HALO + at] = south_ref[0, at].astype(F32)
    x_ref[HALO : HALO + rows, :, :cols] = tr_ref[0]
    for r in range(rows):
        x_ref[HALO + r] = with_columns(x_ref[HALO + r], r, sides, cols, lanes)
    u, v = u_ref[0], v_ref[0]
    face_u = 0.5 * (u + pltpu.roll(u, LANES - 1, 1))
    east_up, east_down = COURANT * jnp.maximum(face_u, 0.0), COURANT * jnp.minimum(face_u, 0.0)
    face_v = 0.5 * (v + pltpu.roll(v, deep - 1, 0))
    row = first_ref[0] - HALO + lax.broadcasted_iota(jnp.int32, face_v.shape, 0)
    face_v = jnp.where((row >= 0) & (row + 1 <= total_rows - 1), face_v, 0.0)
    south_up, south_down = COURANT * jnp.maximum(face_v, 0.0), COURANT * jnp.minimum(face_v, 0.0)
    coef_ref[0] = 1.0 - east_up + pltpu.roll(east_down, 1, 1) - south_up + pltpu.roll(south_down, 1, 0)
    coef_ref[1] = -east_down
    coef_ref[2] = pltpu.roll(east_up, 1, 1)
    coef_ref[3] = -south_down
    coef_ref[4] = pltpu.roll(south_up, 1, 0)
    react = react_ref[...]

    def moved(src, r):
        q = src[r]
        return (
            coef_ref[0, r : r + 1] * q
            + coef_ref[1, r : r + 1] * pltpu.roll(q, LANES - 1, 1)
            + coef_ref[2, r : r + 1] * pltpu.roll(q, 1, 1)
            + coef_ref[3, r : r + 1] * src[r + 1]
            + coef_ref[4, r : r + 1] * src[r - 1]
        )

    def step(src, r):
        both = jnp.concatenate([moved(src, r), moved(src, r + 1)], axis=1)
        high = both.astype(BF)
        low = (both - high.astype(F32)).astype(BF)
        return both + jnp.dot(react, jnp.concatenate([high, high, low], axis=0), preferred_element_type=F32)

    for r in range(1, deep - 1, 2):
        both = step(x_ref, r)
        y_ref[r] = both[:, :LANES]
        y_ref[r + 1] = both[:, LANES:]
    heat = jnp.broadcast_to(heat_ref[...], (tracers, LANES))
    heating_ref[0] = jnp.zeros_like(heating_ref[0])
    for r in range(HALO, rows + HALO, 2):
        both = step(y_ref, r)
        for at in range(2):
            one = both[:, at * LANES : (at + 1) * LANES]
            mix_ref[0, r - HALO + at] = one[:, :cols]
            warm = jnp.sum(heat * one, axis=0, keepdims=True)
            heating_ref[0, r + at : r + at + 1] = jnp.where(lanes[:1] < cols, warm, 0.0)


def shift(value, axis, by):
    count = lax.axis_size(axis)
    return lax.ppermute(value, axis, [(i, (i + by) % count) for i in range(count)])


def edge_columns(tracers):
    levels, rows, count, cols = tracers.shape
    pair = levels // 4
    return pl.pallas_call(
        edge_columns_kernel,
        grid=(levels // pair,),
        in_specs=[pl.BlockSpec((pair, rows, count, cols), lambda l: (l, 0, 0, 0))],
        out_specs=[pl.BlockSpec((pair, count, LANES), lambda l: (l, 0, 0))] * 2,
        out_shape=[jax.ShapeDtypeStruct((levels, count, LANES), BF)] * 2,
        scratch_shapes=[pltpu.VMEM((pair, rows, count, LANES), F32)],
        cost_estimate=pl.CostEstimate(flops=10**7, bytes_accessed=7 * 10**6, transcendentals=0),
        name="edge_columns",
    )(tracers)


def edge_rows(tracers, west, east):
    levels, rows, count, cols = tracers.shape
    row_shape = jax.ShapeDtypeStruct((levels, HALO, count, LANES), BF)
    some = levels // 2
    return pl.pallas_call(
        functools.partial(edge_rows_kernel, rows),
        grid=(levels // some,),
        in_specs=[
            pl.BlockSpec((some, HALO, count, cols), lambda l: (l, 0, 0, 0)),
            pl.BlockSpec((some, HALO, count, cols), lambda l: (l, rows // HALO - 1, 0, 0)),
            pl.BlockSpec((some, count, LANES), lambda l: (l, 0, 0)),
            pl.BlockSpec((some, count, LANES), lambda l: (l, 0, 0)),
        ],
        out_specs=[pl.BlockSpec((some, HALO, count, LANES), lambda l: (l, 0, 0, 0))] * 2,
        scratch_shapes=[pltpu.VMEM((count, LANES), F32)],
        out_shape=[row_shape] * 2,
        cost_estimate=pl.CostEstimate(flops=10**6, bytes_accessed=2 * 10**6, transcendentals=0),
        name="edge_rows",
    )(tracers, tracers, west, east)


def chemistry(tracers, halos, winds, reaction, heat_coeff, row_first, total_rows):
    levels, rows, count, cols = tracers.shape
    deep = rows + 2 * HALO
    high = reaction.astype(BF)
    low = (reaction - high.astype(F32)).astype(BF)
    react = jnp.concatenate([high, low, high], axis=1)
    heat = heat_coeff[:, None]
    tr_spec = pl.BlockSpec((1, rows, count, cols), lambda l: (l, 0, 0, 0))
    col_spec = pl.BlockSpec((1, count, LANES), lambda l: (l, 0, 0))
    row_spec = pl.BlockSpec((1, HALO, count, LANES), lambda l: (l, 0, 0, 0))
    whole = lambda shape: pl.BlockSpec(shape, lambda l: (0,) * len(shape))
    return pl.pallas_call(
        functools.partial(chemistry_kernel, total_rows),
        grid=(levels,),
        in_specs=[
            pl.BlockSpec(memory_space=pltpu.SMEM),
            tr_spec,
            row_spec,
            row_spec,
            col_spec,
            col_spec,
            pl.BlockSpec((1, deep, LANES), lambda l: (l, 0, 0)),
            pl.BlockSpec((1, deep, LANES), lambda l: (l + levels, 0, 0)),
            whole(react.shape),
            whole(heat.shape),
        ],
        out_specs=[tr_spec, pl.BlockSpec((1, deep, LANES), lambda l: (l, 0, 0))],
        out_shape=[
            jax.ShapeDtypeStruct(tracers.shape, F32),
            jax.ShapeDtypeStruct((levels, deep, LANES), F32),
        ],
        scratch_shapes=[
            pltpu.VMEM((deep, count, LANES), F32),
            pltpu.VMEM((deep, count, LANES), F32),
            pltpu.VMEM((5, deep, LANES), F32),
        ],
        cost_estimate=pl.CostEstimate(flops=10**9, bytes_accessed=16 * 10**6, transcendentals=0),
        name="chemistry",
    )(row_first.reshape(1), tracers, *halos, winds, winds, react, heat)


def body(spectra, legendre, gauss_weights, phys_matrix, phys_bias, tracers, reaction, heat_coeff):
    waves = lax.axis_size("wave")
    levs = lax.axis_size("lev")
    both = ("wave", "lev")
    wave, lev = lax.axis_index("wave"), lax.axis_index("lev")
    m_count, k_count, _, fields = spectra.shape
    half_rows = legendre.shape[1]
    levels, _, chem_rows, chem_cols = tracers.shape
    ratio = NLON // (chem_cols * levs)
    bands = waves // 2
    groups = (chem_rows + 2 * HALO) // levs
    width = 2 * fields

    owners = waves * levs
    geometry = (waves, levs, groups, bands, chem_rows, m_count)
    first_m = (wave * levs + lev) * m_count
    piece_shape = (owners, PIECE_ROWS, LANES)
    piece_spec = pl.BlockSpec(piece_shape, lambda m: (0, 0, 0))
    spec_spec = pl.BlockSpec((1, width, k_count), lambda m: (m, 0, 0))
    used = groups * 2 * m_count
    tracers = tracers.transpose(0, 2, 1, 3)

    pieces = legendre_call(
        inverse_kernel,
        "to_latitude",
        2,
        first_m,
        [spectra.transpose(0, 2, 3, 1).reshape(m_count, width, k_count)],
        [spec_spec],
        piece_spec,
        jax.ShapeDtypeStruct(piece_shape, BF),
        geometry,
        legendre,
    )
    spread = lax.all_to_all(pieces, both, split_axis=0, concat_axis=0, tiled=True)
    head, tail = edge_columns(tracers)
    west, east = shift(tail, "lev", 1), shift(head, "lev", -1)
    table = fourier_table(owners, m_count)
    spread = spread[:, :used].transpose(1, 0, 2)
    tiles = groups * 2 * UNIT
    spread = jnp.concatenate(
        [spread[:tiles].reshape(groups, 2, UNIT, owners, LANES), spread[tiles:].reshape(groups, 2, -1, owners, LANES)],
        axis=2,
    ).reshape(groups, 2, TRUNC, LANES)

    sums = jnp.einsum("gckn,ckj->cgnj", spread, table.reshape(2, TRUNC, FOLD), preferred_element_type=F32)
    cosine, sine, turn = sums[0, ..., :HALF], sums[1, ..., :HALF], sums[0, ..., HALF : HALF + 1]
    turned = jnp.where(jnp.arange(HALF, dtype=jnp.int32) == 0, turn, cosine - sine)
    halves = [value.astype(BF).reshape(groups, ratio, fields, HALF) for value in (cosine + sine, turned)]

    lane = jnp.arange(LANES, dtype=jnp.int32)
    column = jnp.where(lane < LANES - HALO, lane, lane - LANES)
    column = (column[None, :] + chem_cols * jnp.arange(levs, dtype=jnp.int32)[:, None]) % (chem_cols * levs)
    held = (lane < chem_cols + HALO) | (lane >= LANES - HALO)
    column = jnp.where(held[None, :], column, -1).reshape(levs * LANES)
    order = jnp.arange(HALF, dtype=jnp.int32)
    cells = [order // ratio, jnp.where(order == 0, HALF, NLON - order) // ratio]
    means = [jnp.where(cell[:, None] == column[None, :], 1.0 / ratio**2, 0.0).astype(BF) for cell in cells]
    cell = jnp.concatenate(cells)
    winds = sum(
        jnp.einsum("gqfj,jx->gqfx", half[:, :, : 2 * levels], part, preferred_element_type=F32).sum(axis=1)
        for half, part in zip(halves, means)
    )
    winds = winds.reshape(groups * 2 * levels, levs, LANES).transpose(1, 0, 2)
    winds, west, east = lax.optimization_barrier((winds, west, east))
    top, low = edge_rows(tracers, west, east)
    halos = (shift(low, "wave", 1), shift(top, "wave", -1), west, east)
    winds = lax.all_to_all(winds, "lev", split_axis=0, concat_axis=0, tiled=True)
    winds = winds.reshape(levs * groups, 2 * levels, LANES).transpose(1, 0, 2)

    mixing, heating = chemistry(
        tracers, halos, winds, reaction, heat_coeff, wave * chem_rows, chem_rows * waves
    )
    heating = heating.transpose(1, 0, 2).reshape(levs, groups * levels, LANES)
    heating = lax.all_to_all(heating, "lev", split_axis=0, concat_axis=0, tiled=True)
    heating = heating.transpose(1, 0, 2).reshape(groups * levels, levs * LANES)
    high = heating.astype(BF)
    low = (heating - high.astype(F32)).astype(BF)
    column = jnp.where(lane[None, :] < chem_cols, lane + chem_cols * jnp.arange(levs, dtype=jnp.int32)[:, None], -1)
    copied = (column.reshape(levs * LANES)[:, None] == cell[None, :]).astype(BF)
    heating = jnp.dot(jnp.concatenate([high, low]), copied, preferred_element_type=F32)

    values, warm = [], []
    for half in halves:
        physics = jnp.tanh(
            jnp.einsum("ef,gqfj->gqej", phys_matrix, half.astype(F32), precision=lax.Precision.HIGHEST)
            + phys_bias[:, None]
        )
        values.append(physics.astype(BF).reshape(groups * ratio * fields, HALF))
        warm.append(physics[:, :, 2 * levels : 3 * levels].reshape(groups * ratio * levels, HALF))

    coeffs = grid_to_pieces(table, values, warm, heating, owners)
    values = lax.all_to_all(coeffs, both, split_axis=0, concat_axis=0, tiled=True)

    result = legendre_call(
        direct_kernel,
        "to_spectral",
        2,
        first_m,
        [values, gauss_weights.reshape(half_rows // 4, 4)],
        [piece_spec, pl.BlockSpec((half_rows // 4, 4), lambda m: (0, 0))],
        spec_spec,
        jax.ShapeDtypeStruct((m_count, width, k_count), BF),
        geometry,
        legendre,
    )
    result = result.reshape(m_count, 2, fields, k_count).transpose(0, 3, 1, 2)
    mixing = mixing.transpose(0, 2, 1, 3)
    return (result, mixing)


def solution(mesh):
    return jax.shard_map(
        body,
        mesh=mesh,
        in_specs=(
            P(("wave", "lev"), None, None, None),
            P(("wave", "lev"), None, None),
            P(),
            P(),
            P(),
            P(None, None, "wave", "lev"),
            P(),
            P(),
        ),
        out_specs=(P(("wave", "lev"), None, None, None), P(None, None, "wave", "lev")),
        check_vma=False,
    )
```

```python
import functools
import math

import jax
import jax.numpy as jnp
from jax import lax
from jax.experimental import pallas as pl
from jax.experimental.pallas import tpu as pltpu
from jax.sharding import PartitionSpec as P

TRUNC = 1280
NLON = 2560
HALF = NLON // 2
SUBSTEPS = 2
COURANT = 0.6
LANES = 128
FOLD = HALF + LANES
PIECE_ROWS = 64
DEPTH = 3
UNIT = 8
HALO = 2
BF, F32 = jnp.bfloat16, jnp.float32


def table_kernel(cos_ref, sin_ref, turned_cos_ref, turned_sin_ref, a_ref, b_ref, out_ref):
    step = pl.program_id(0)
    owners = cos_ref.shape[0]
    for row in range(a_ref.shape[0]):
        for block in range(FOLD // LANES):
            part = slice(block * LANES, (block + 1) * LANES)
            cos, sin = (turned_cos_ref, turned_sin_ref) if block % 2 else (cos_ref, sin_ref)
            value = cos[...] * a_ref[row, :, part] - sin[...] * b_ref[row, :, part]
            out_ref[row * owners : (row + 1) * owners, part] = value.astype(BF)

    @pl.when(step == 0)
    def _():
        top = out_ref[:16, :].astype(F32)
        first = lax.broadcasted_iota(jnp.int32, top.shape, 0) == 0
        out_ref[:16, :] = jnp.where(first, 0.5 * top, top).astype(BF)


def fourier_table(owners, m_count):
    unit = 2.0 * math.pi / NLON
    owner = jnp.arange(owners, dtype=jnp.int32)[:, None]
    lane = jnp.arange(LANES, dtype=jnp.int32)[None, :]
    coarse = (m_count * owner * lane % NLON).astype(F32) * unit
    cos_c, sin_c = jnp.cos(coarse), jnp.sin(coarse)
    turn = jnp.where(owner % 2 == 1, -1.0, 1.0).astype(F32)
    inner = jnp.arange(m_count, dtype=jnp.int32)[:, None]
    fine = (inner * jnp.arange(FOLD, dtype=jnp.int32)[None, :] % NLON).astype(F32) * unit
    cos, sin = jnp.cos(fine), jnp.sin(fine)
    a = 2.0 * jnp.concatenate([cos, -sin])
    b = 2.0 * jnp.concatenate([sin, cos])
    rows = 2 * m_count
    coarse_spec = pl.BlockSpec((owners, LANES), lambda i: (0, 0))
    fine_spec = pl.BlockSpec((PARTS, 1, FOLD), lambda i: (i, 0, 0))
    out_spec = pl.BlockSpec((PARTS * owners, FOLD), lambda i: (i, 0))
    shape = jax.ShapeDtypeStruct((owners * rows, FOLD), BF)
    return pl.pallas_call(
        table_kernel,
        grid=(rows // PARTS,),
        in_specs=[coarse_spec] * 4 + [fine_spec] * 2,
        out_specs=out_spec,
        out_shape=shape,
        cost_estimate=pl.CostEstimate(flops=6 * TRUNC * FOLD, bytes_accessed=4 * TRUNC * FOLD, transcendentals=0),
        name="fourier_table",
    )(cos_c, sin_c, turn * cos_c, turn * sin_c, a[:, None], b[:, None])


def exchanged(x, turned):
    lanes = lane_ids(x[0].shape)
    low, even = lanes < 64, (lanes & 32) == 0
    pairs = [(jnp.where(low, x[i], turned[i + 2]), jnp.where(low, turned[i], x[i + 2])) for i in range(2)]
    out = []
    for first, second in zip(*pairs):
        out.append(jnp.where(even, first, pltpu.roll(second, 32, 1)))
        out.append(jnp.where(even, pltpu.roll(first, LANES - 32, 1), second))
    return out


def kept(m, shape, part_rows):
    row = lax.broadcasted_iota(jnp.int32, shape, 0)
    k = lax.broadcasted_iota(jnp.int32, shape, 1)
    return (k < TRUNC - m) & ((row < part_rows) | (m > 0)), k % 2 == 0


def table_copy(leg_ref, table_ref, sem, m):
    slot = m % DEPTH
    return pltpu.make_async_copy(leg_ref.at[m], table_ref.at[slot], sem.at[slot])


def start_copies(leg_ref, table_ref, sem, step, count):
    @pl.when(step == 0)
    def _():
        for m in range(DEPTH - 1):
            table_copy(leg_ref, table_ref, sem, m).start()

    @pl.when(step + DEPTH - 1 < count)
    def _():
        table_copy(leg_ref, table_ref, sem, step + DEPTH - 1).start()


def inverse_kernel(geometry, first_ref, spec_ref, leg_ref, out_ref, z_ref, q_ref, x_ref, turned_ref, table_ref, sem):
    waves, levs, groups, bands, band_groups, m_count = geometry
    half_rows = leg_ref.shape[1]
    step = pl.program_id(0)
    start_copies(leg_ref, table_ref, sem, step, m_count)
    spec = spec_ref[0].astype(F32)
    keep, even = kept(first_ref[0] + step, spec.shape, spec.shape[0] // 2)
    spec = jnp.where(keep, spec, 0.0)
    other = jnp.where(even, spec, -spec)
    stacked = jnp.concatenate([spec, other, other, spec], axis=0).astype(BF)
    table_copy(leg_ref, table_ref, sem, step).wait()
    values = lax.dot_general(table_ref[step % DEPTH], stacked, (((1,), (1,)), ((), ())), preferred_element_type=F32)
    x_ref[...] = values[:, :LANES]
    turned_ref[...] = values[:, LANES:]
    quarter = half_rows // 4
    lines = [pl.ds(q, quarter, stride=4) for q in range(4)]
    for part, value in enumerate(exchanged([x_ref[i, :] for i in lines], [turned_ref[i, :] for i in lines])):
        z_ref[pl.ds(step * half_rows + part * quarter, quarter), :] = value

    @pl.when(step == m_count - 1)
    def _():
        q_ref[...] = jnp.zeros_like(q_ref)

        def of_wave(wave, carry):
            south = (wave >= bands).astype(jnp.int32)
            band = jnp.where(wave >= bands, waves - 1 - wave, wave)
            for lev in range(levs):
                for g in range(groups):
                    slot = lev * groups + g
                    at = band * band_groups + jnp.where(south == 1, band_groups + HALO - 1 - slot, slot - HALO)
                    over = at >= bands * band_groups
                    line = jnp.where(over, 2 * bands * band_groups - 1 - at, jnp.maximum(at, 0))
                    base = line + jnp.where(over, 1 - south, south) * (half_rows // 2)
                    for c in range(2):
                        for row, count, skip in moves(geometry, half_rows, slot, c):
                            start = base + (c * (half_rows // 4) + skip)
                            q_ref[lev, row : row + count] = z_ref[pl.ds(start, count, stride=half_rows), :]
                out_ref[wave * levs + lev] = q_ref[lev].astype(BF)
            return carry

        lax.fori_loop(0, waves, of_wave, 0)


def direct_kernel(geometry, first_ref, values_ref, weights_ref, leg_ref, out_ref, z_ref, q_ref, x_ref, w_ref, table_ref, sem):
    waves, levs, groups, bands, band_groups, m_count = geometry
    half_rows = leg_ref.shape[1]
    step = pl.program_id(0)
    start_copies(leg_ref, table_ref, sem, step, m_count)

    @pl.when(step == 0)
    def _():
        for q in range(4):
            rows = pl.ds(q * (half_rows // 4), half_rows // 4)
            w_ref[rows, :] = jnp.broadcast_to(weights_ref[:, q : q + 1], (half_rows // 4, LANES))

        def of_wave(wave, carry):
            south = (wave >= bands).astype(jnp.int32)
            band = jnp.where(wave >= bands, waves - 1 - wave, wave)
            for lev in range(levs):
                q_ref[lev] = values_ref[wave * levs + lev].astype(F32)
                for g in range(groups):
                    slot = lev * groups + g
                    if HALO <= slot < band_groups + HALO:
                        inside = jnp.where(south == 1, band_groups + HALO - 1 - slot, slot - HALO)
                        base = band * band_groups + inside + south * (half_rows // 2)
                        for c in range(2):
                            for row, count, skip in moves(geometry, half_rows, slot, c):
                                start = base + (c * (half_rows // 4) + skip)
                                z_ref[pl.ds(start, count, stride=half_rows), :] = q_ref[lev, row : row + count]
            return carry

        lax.fori_loop(0, waves, of_wave, 0)

    quarter = half_rows // 4
    x = [z_ref[pl.ds(step * half_rows + part * quarter, quarter), :] for part in range(4)]
    x = [x[0] + x[2], x[1] + x[3], x[0] - x[2], x[1] - x[3]]
    for q, value in enumerate(exchanged(x, [pltpu.roll(i, 64, 1) for i in x])):
        x_ref[pl.ds(q, quarter, stride=4), :] = w_ref[pl.ds(q * quarter, quarter), :] * value
    paired = x_ref[...].astype(BF)
    table_copy(leg_ref, table_ref, sem, step).wait()
    folded = lax.dot_general(paired, table_ref[step % DEPTH], (((0,), (0,)), ((), ())), preferred_element_type=F32)
    half = folded.shape[0] // 2
    keep, even = kept(first_ref[0] + step, (half, folded.shape[1]), half // 2)
    chosen = jnp.where(even, folded[:half], folded[half:])
    out_ref[0] = jnp.where(keep, chosen, 0.0).astype(BF)


def moves(geometry, half_rows, slot, c):
    m_count = geometry[-1]
    units = 2 * geometry[2]
    unit = 2 * (slot % geometry[2]) + c
    tail = m_count - UNIT
    return (unit * UNIT, UNIT, 0), (units * UNIT + unit * tail, tail, UNIT * half_rows)


def legendre_call(kernel, name, extra, first, operands, in_specs, out_spec, out_shape, geometry, legendre):
    m_count, half_rows, k_count = legendre.shape
    levs = geometry[1]
    return pl.pallas_call(
        functools.partial(kernel, geometry),
        grid=(m_count,),
        in_specs=[pl.BlockSpec(memory_space=pltpu.SMEM)]
        + in_specs
        + [pl.BlockSpec(memory_space=pl.ANY)],
        out_specs=out_spec,
        out_shape=out_shape,
        scratch_shapes=[
            pltpu.VMEM((m_count * half_rows, LANES), F32),
            pltpu.VMEM((levs, PIECE_ROWS, LANES), F32),
        ]
        + [pltpu.VMEM((half_rows, LANES), F32)] * extra
        + [pltpu.VMEM((DEPTH, half_rows, k_count), BF), pltpu.SemaphoreType.DMA((DEPTH,))],
        cost_estimate=pl.CostEstimate(
            flops=2 * legendre.size * LANES, bytes_accessed=2 * legendre.size + 5 * 10**6, transcendentals=0
        ),
        name=name,
    )(first.reshape(1), *operands, legendre)


PARTS = 5


def grid_kernel(owners, steps, table_ref, *refs):
    value_refs, warm_refs, (heat_ref, out_ref, pack_ref, fold_ref) = refs[:2], refs[2:4], refs[4:]
    step = pl.program_id(0)
    lines = value_refs[0].shape[0]
    groups = lines // LANES
    rows = out_ref.shape[1]
    m_count = steps * PARTS // 2

    @pl.when(step == 0)
    def _():
        scale = 0.5 / math.sqrt(NLON)
        start = lane_ids((lines, LANES)) == 0
        columns = lines // 32
        levels = warm_refs[0].shape[0] // columns
        below = heat_ref.shape[0] // 2

        def tendency(side, block):
            part = slice(block * LANES, (block + 1) * LANES)
            there = slice(side * HALF + block * LANES, side * HALF + (block + 1) * LANES)
            value = value_refs[side][:, part].astype(F32)
            pieces = []
            for at in range(columns):
                cell = at // (columns // groups) * levels
                heat = heat_ref[cell : cell + levels, there] + heat_ref[below + cell : below + cell + levels, there]
                warm = warm_refs[side][at * levels : (at + 1) * levels, part] + heat
                pieces += [value[at * 32 : at * 32 + 2 * levels], warm.astype(BF).astype(F32)]
                pieces += [value[at * 32 + 3 * levels : (at + 1) * 32]]
            return jnp.concatenate(pieces, axis=0)

        for block in range(HALF // LANES):
            west, east = tendency(0, block), tendency(1, block)
            total = west + east
            if block == 0:
                total = jnp.where(start, west, total)
                fold_ref[0, :, HALF:] = jnp.where(start, scale * east, 0.0).astype(BF)
                fold_ref[1, :, HALF:] = jnp.zeros((lines, LANES), BF)
            fold_ref[0, :, block * LANES : (block + 1) * LANES] = (scale * total).astype(BF)
            fold_ref[1, :, block * LANES : (block + 1) * LANES] = (scale * (west - east)).astype(BF)

    part_c = step // (steps // 2)
    result = lax.dot_general(
        table_ref[...], fold_ref[part_c], (((1,), (1,)), ((), ())), preferred_element_type=F32
    )
    first = (lax.broadcasted_iota(jnp.int32, (owners, LANES), 0) == 0) & (step == 0)
    tail = m_count - UNIT
    for part in range(PARTS):
        m = step % (steps // 2) * PARTS + part
        for g in range(groups):
            unit = 2 * g + part_c
            start = jnp.where(m < UNIT, unit * UNIT + m, 2 * groups * UNIT + unit * tail + m - UNIT)
            value = result[part * owners : (part + 1) * owners, g * LANES : (g + 1) * LANES]
            if part == 0:
                value = jnp.where(first, 2.0 * value, value)
            pack_ref[pl.ds(start, owners, stride=rows), :] = value

    @pl.when(step == steps - 1)
    def _():
        blank = jnp.zeros((owners, LANES), F32)
        for row in range(groups * PARTS * steps, rows):
            pack_ref[pl.ds(row, owners, stride=rows), :] = blank
        out_ref[...] = pack_ref[...].reshape(out_ref.shape).astype(BF)


def grid_to_pieces(table, values, warm, heating, owners):
    steps = table.shape[0] // owners // PARTS
    return pl.pallas_call(
        functools.partial(grid_kernel, owners, steps),
        grid=(steps,),
        in_specs=[
            pl.BlockSpec((PARTS * owners, FOLD), lambda i: (i, 0)),
            *[pl.BlockSpec(value.shape, lambda i: (0, 0)) for value in (*values, *warm, heating)],
        ],
        out_specs=pl.BlockSpec((owners, PIECE_ROWS, LANES), lambda i: (0, 0, 0)),
        out_shape=jax.ShapeDtypeStruct((owners, PIECE_ROWS, LANES), BF),
        scratch_shapes=[
            pltpu.VMEM((owners * PIECE_ROWS, LANES), F32),
            pltpu.VMEM((2, values[0].shape[0], FOLD), BF),
        ],
        cost_estimate=pl.CostEstimate(
            flops=2 * table.size * values[0].shape[0], bytes_accessed=2 * table.size + 5 * 10**6, transcendentals=0
        ),
        name="grid_to_pieces",
    )(table, *values, *warm, heating)


def lane_ids(shape):
    return lax.broadcasted_iota(jnp.int32, shape, len(shape) - 1)


def edge_columns_kernel(tr_ref, head_ref, tail_ref, pad):
    levels, rows, count, cols = tr_ref.shape
    lanes = lane_ids((count, LANES))
    gap = LANES - HALO - cols
    for level in range(levels):
        head = jnp.zeros((count, LANES), F32)
        tail = head
        pad[level, :, :, :cols] = tr_ref[level]
        for r in range(rows):
            line = pad[level, r]
            head = jnp.where((lanes >> 1) == r, pltpu.roll(line, 2 * r, 1), head)
            tail = jnp.where(
                (lanes >> 1) == r + gap // 2, pltpu.roll(line, (2 * r + gap - cols + HALO) % LANES, 1), tail
            )
        head_ref[level] = head.astype(BF)
        tail_ref[level] = tail.astype(BF)


def both_sides(west, east, cols, lanes):
    return jnp.where(lanes < LANES - HALO - cols, east.astype(F32), west.astype(F32))


def with_columns(line, r, sides, cols, lanes):
    here = ((lanes >> 1) == cols // 2) | ((lanes >> 1) == LANES // 2 - 1)
    return jnp.where(here, pltpu.roll(sides, (cols - 2 * r) % LANES, 1), line)


def edge_rows_kernel(rows, first_ref, last_ref, west_ref, east_ref, top_ref, low_ref, line):
    levels, _, count, cols = first_ref.shape
    lanes = lane_ids((count, LANES))
    for level in range(levels):
        sides = both_sides(west_ref[level], east_ref[level], cols, lanes)
        for at in range(HALO):
            for src, out, r in ((first_ref, top_ref, at), (last_ref, low_ref, rows - HALO + at)):
                line[:, :cols] = src[level, at]
                out[level, at] = with_columns(line[...], r, sides, cols, lanes).astype(BF)


def chemistry_kernel(
    total_rows, first_ref, tr_ref, north_ref, south_ref, west_ref, east_ref, u_ref, v_ref, react_ref, heat_ref,
    mix_ref, heating_ref, x_ref, y_ref, coef_ref,
):
    rows, tracers, cols = tr_ref.shape[1:]
    deep = rows + 2 * HALO
    lanes = lane_ids((tracers, LANES))
    sides = both_sides(west_ref[0], east_ref[0], cols, lanes)
    for at in range(HALO):
        x_ref[at] = north_ref[0, at].astype(F32)
        x_ref[rows + HALO + at] = south_ref[0, at].astype(F32)
    x_ref[HALO : HALO + rows, :, :cols] = tr_ref[0]
    for r in range(rows):
        x_ref[HALO + r] = with_columns(x_ref[HALO + r], r, sides, cols, lanes)
    u, v = u_ref[0], v_ref[0]
    face_u = 0.5 * (u + pltpu.roll(u, LANES - 1, 1))
    east_up, east_down = COURANT * jnp.maximum(face_u, 0.0), COURANT * jnp.minimum(face_u, 0.0)
    face_v = 0.5 * (v + pltpu.roll(v, deep - 1, 0))
    row = first_ref[0] - HALO + lax.broadcasted_iota(jnp.int32, face_v.shape, 0)
    face_v = jnp.where((row >= 0) & (row + 1 <= total_rows - 1), face_v, 0.0)
    south_up, south_down = COURANT * jnp.maximum(face_v, 0.0), COURANT * jnp.minimum(face_v, 0.0)
    coef_ref[0] = 1.0 - east_up + pltpu.roll(east_down, 1, 1) - south_up + pltpu.roll(south_down, 1, 0)
    coef_ref[1] = -east_down
    coef_ref[2] = pltpu.roll(east_up, 1, 1)
    coef_ref[3] = -south_down
    coef_ref[4] = pltpu.roll(south_up, 1, 0)
    react = react_ref[...]

    def moved(src, r):
        q = src[r]
        return (
            coef_ref[0, r : r + 1] * q
            + coef_ref[1, r : r + 1] * pltpu.roll(q, LANES - 1, 1)
            + coef_ref[2, r : r + 1] * pltpu.roll(q, 1, 1)
            + coef_ref[3, r : r + 1] * src[r + 1]
            + coef_ref[4, r : r + 1] * src[r - 1]
        )

    def step(src, r):
        both = jnp.concatenate([moved(src, r), moved(src, r + 1)], axis=1)
        high = both.astype(BF)
        low = (both - high.astype(F32)).astype(BF)
        return both + jnp.dot(react, jnp.concatenate([high, high, low], axis=0), preferred_element_type=F32)

    for r in range(1, deep - 1, 2):
        both = step(x_ref, r)
        y_ref[r] = both[:, :LANES]
        y_ref[r + 1] = both[:, LANES:]
    heat = jnp.broadcast_to(heat_ref[...], (tracers, LANES))
    heating_ref[0] = jnp.zeros_like(heating_ref[0])
    for r in range(HALO, rows + HALO, 2):
        both = step(y_ref, r)
        for at in range(2):
            one = both[:, at * LANES : (at + 1) * LANES]
            mix_ref[0, r - HALO + at] = one[:, :cols]
            warm = jnp.sum(heat * one, axis=0, keepdims=True)
            heating_ref[0, r + at : r + at + 1] = jnp.where(lanes[:1] < cols, warm, 0.0)


def shift(value, axis, by):
    count = lax.axis_size(axis)
    return lax.ppermute(value, axis, [(i, (i + by) % count) for i in range(count)])


def edge_columns(tracers):
    levels, rows, count, cols = tracers.shape
    pair = levels // 4
    return pl.pallas_call(
        edge_columns_kernel,
        grid=(levels // pair,),
        in_specs=[pl.BlockSpec((pair, rows, count, cols), lambda l: (l, 0, 0, 0))],
        out_specs=[pl.BlockSpec((pair, count, LANES), lambda l: (l, 0, 0))] * 2,
        out_shape=[jax.ShapeDtypeStruct((levels, count, LANES), BF)] * 2,
        scratch_shapes=[pltpu.VMEM((pair, rows, count, LANES), F32)],
        cost_estimate=pl.CostEstimate(flops=10**7, bytes_accessed=7 * 10**6, transcendentals=0),
        name="edge_columns",
    )(tracers)


def edge_rows(tracers, west, east):
    levels, rows, count, cols = tracers.shape
    row_shape = jax.ShapeDtypeStruct((levels, HALO, count, LANES), BF)
    some = levels // 2
    return pl.pallas_call(
        functools.partial(edge_rows_kernel, rows),
        grid=(levels // some,),
        in_specs=[
            pl.BlockSpec((some, HALO, count, cols), lambda l: (l, 0, 0, 0)),
            pl.BlockSpec((some, HALO, count, cols), lambda l: (l, rows // HALO - 1, 0, 0)),
            pl.BlockSpec((some, count, LANES), lambda l: (l, 0, 0)),
            pl.BlockSpec((some, count, LANES), lambda l: (l, 0, 0)),
        ],
        out_specs=[pl.BlockSpec((some, HALO, count, LANES), lambda l: (l, 0, 0, 0))] * 2,
        scratch_shapes=[pltpu.VMEM((count, LANES), F32)],
        out_shape=[row_shape] * 2,
        cost_estimate=pl.CostEstimate(flops=10**6, bytes_accessed=2 * 10**6, transcendentals=0),
        name="edge_rows",
    )(tracers, tracers, west, east)


def chemistry(tracers, halos, winds, reaction, heat_coeff, row_first, total_rows):
    levels, rows, count, cols = tracers.shape
    deep = rows + 2 * HALO
    high = reaction.astype(BF)
    low = (reaction - high.astype(F32)).astype(BF)
    react = jnp.concatenate([high, low, high], axis=1)
    heat = heat_coeff[:, None]
    tr_spec = pl.BlockSpec((1, rows, count, cols), lambda l: (l, 0, 0, 0))
    col_spec = pl.BlockSpec((1, count, LANES), lambda l: (l, 0, 0))
    row_spec = pl.BlockSpec((1, HALO, count, LANES), lambda l: (l, 0, 0, 0))
    whole = lambda shape: pl.BlockSpec(shape, lambda l: (0,) * len(shape))
    return pl.pallas_call(
        functools.partial(chemistry_kernel, total_rows),
        grid=(levels,),
        in_specs=[
            pl.BlockSpec(memory_space=pltpu.SMEM),
            tr_spec,
            row_spec,
            row_spec,
            col_spec,
            col_spec,
            pl.BlockSpec((1, deep, LANES), lambda l: (l, 0, 0)),
            pl.BlockSpec((1, deep, LANES), lambda l: (l + levels, 0, 0)),
            whole(react.shape),
            whole(heat.shape),
        ],
        out_specs=[tr_spec, pl.BlockSpec((1, deep, LANES), lambda l: (l, 0, 0))],
        out_shape=[
            jax.ShapeDtypeStruct(tracers.shape, F32),
            jax.ShapeDtypeStruct((levels, deep, LANES), F32),
        ],
        scratch_shapes=[
            pltpu.VMEM((deep, count, LANES), F32),
            pltpu.VMEM((deep, count, LANES), F32),
            pltpu.VMEM((5, deep, LANES), F32),
        ],
        cost_estimate=pl.CostEstimate(flops=10**9, bytes_accessed=16 * 10**6, transcendentals=0),
        name="chemistry",
    )(row_first.reshape(1), tracers, *halos, winds, winds, react, heat)


def body(spectra, legendre, gauss_weights, phys_matrix, phys_bias, tracers, reaction, heat_coeff):
    waves = lax.axis_size("wave")
    levs = lax.axis_size("lev")
    both = ("wave", "lev")
    wave, lev = lax.axis_index("wave"), lax.axis_index("lev")
    m_count, k_count, _, fields = spectra.shape
    half_rows = legendre.shape[1]
    levels, _, chem_rows, chem_cols = tracers.shape
    ratio = NLON // (chem_cols * levs)
    bands = waves // 2
    groups = (chem_rows + 2 * HALO) // levs
    width = 2 * fields

    owners = waves * levs
    geometry = (waves, levs, groups, bands, chem_rows, m_count)
    first_m = (wave * levs + lev) * m_count
    piece_shape = (owners, PIECE_ROWS, LANES)
    piece_spec = pl.BlockSpec(piece_shape, lambda m: (0, 0, 0))
    spec_spec = pl.BlockSpec((1, width, k_count), lambda m: (m, 0, 0))
    used = groups * 2 * m_count
    tracers = tracers.transpose(0, 2, 1, 3)

    pieces = legendre_call(
        inverse_kernel,
        "to_latitude",
        2,
        first_m,
        [spectra.transpose(0, 2, 3, 1).reshape(m_count, width, k_count)],
        [spec_spec],
        piece_spec,
        jax.ShapeDtypeStruct(piece_shape, BF),
        geometry,
        legendre,
    )
    spread = lax.all_to_all(pieces, both, split_axis=0, concat_axis=0, tiled=True)
    head, tail = edge_columns(tracers)
    west, east = shift(tail, "lev", 1), shift(head, "lev", -1)
    table = fourier_table(owners, m_count)
    spread = spread[:, :used].transpose(1, 0, 2)
    tiles = groups * 2 * UNIT
    spread = jnp.concatenate(
        [spread[:tiles].reshape(groups, 2, UNIT, owners, LANES), spread[tiles:].reshape(groups, 2, -1, owners, LANES)],
        axis=2,
    ).reshape(groups, 2, TRUNC, LANES)

    sums = jnp.einsum("gckn,ckj->cgnj", spread, table.reshape(2, TRUNC, FOLD), preferred_element_type=F32)
    cosine, sine, turn = sums[0, ..., :HALF], sums[1, ..., :HALF], sums[0, ..., HALF : HALF + 1]
    turned = jnp.where(jnp.arange(HALF, dtype=jnp.int32) == 0, turn, cosine - sine)
    halves = [value.astype(BF).reshape(groups, ratio, fields, HALF) for value in (cosine + sine, turned)]

    lane = jnp.arange(LANES, dtype=jnp.int32)
    column = jnp.where(lane < LANES - HALO, lane, lane - LANES)
    column = (column[None, :] + chem_cols * jnp.arange(levs, dtype=jnp.int32)[:, None]) % (chem_cols * levs)
    held = (lane < chem_cols + HALO) | (lane >= LANES - HALO)
    column = jnp.where(held[None, :], column, -1).reshape(levs * LANES)
    order = jnp.arange(HALF, dtype=jnp.int32)
    cells = [order // ratio, jnp.where(order == 0, HALF, NLON - order) // ratio]
    means = [jnp.where(cell[:, None] == column[None, :], 1.0 / ratio**2, 0.0).astype(BF) for cell in cells]
    cell = jnp.concatenate(cells)
    winds = sum(
        jnp.einsum("gqfj,jx->gqfx", half[:, :, : 2 * levels], part, preferred_element_type=F32).sum(axis=1)
        for half, part in zip(halves, means)
    )
    winds = winds.reshape(groups * 2 * levels, levs, LANES).transpose(1, 0, 2)
    winds, west, east = lax.optimization_barrier((winds, west, east))
    top, low = edge_rows(tracers, west, east)
    halos = (shift(low, "wave", 1), shift(top, "wave", -1), west, east)
    winds = lax.all_to_all(winds, "lev", split_axis=0, concat_axis=0, tiled=True)
    winds = winds.reshape(levs * groups, 2 * levels, LANES).transpose(1, 0, 2)

    mixing, heating = chemistry(
        tracers, halos, winds, reaction, heat_coeff, wave * chem_rows, chem_rows * waves
    )
    heating = heating.transpose(1, 0, 2).reshape(levs, groups * levels, LANES)
    heating = lax.all_to_all(heating, "lev", split_axis=0, concat_axis=0, tiled=True)
    heating = heating.transpose(1, 0, 2).reshape(groups * levels, levs * LANES)
    high = heating.astype(BF)
    low = (heating - high.astype(F32)).astype(BF)
    column = jnp.where(lane[None, :] < chem_cols, lane + chem_cols * jnp.arange(levs, dtype=jnp.int32)[:, None], -1)
    copied = (column.reshape(levs * LANES)[:, None] == cell[None, :]).astype(BF)
    heating = jnp.dot(jnp.concatenate([high, low]), copied, preferred_element_type=F32)

    values, warm = [], []
    for half in halves:
        physics = jnp.tanh(
            jnp.einsum("ef,gqfj->gqej", phys_matrix, half.astype(F32), precision=lax.Precision.HIGHEST)
            + phys_bias[:, None]
        )
        values.append(physics.astype(BF).reshape(groups * ratio * fields, HALF))
        warm.append(physics[:, :, 2 * levels : 3 * levels].reshape(groups * ratio * levels, HALF))

    coeffs = grid_to_pieces(table, values, warm, heating, owners)
    values = lax.all_to_all(coeffs, both, split_axis=0, concat_axis=0, tiled=True)

    result = legendre_call(
        direct_kernel,
        "to_spectral",
        2,
        first_m,
        [values, gauss_weights.reshape(half_rows // 4, 4)],
        [piece_spec, pl.BlockSpec((half_rows // 4, 4), lambda m: (0, 0))],
        spec_spec,
        jax.ShapeDtypeStruct((m_count, width, k_count), BF),
        geometry,
        legendre,
    )
    result = result.reshape(m_count, 2, fields, k_count).transpose(0, 3, 1, 2)
    mixing = mixing.transpose(0, 2, 1, 3)
    return (result, mixing)


def solution(mesh):
    return jax.shard_map(
        body,
        mesh=mesh,
        in_specs=(
            P(("wave", "lev"), None, None, None),
            P(("wave", "lev"), None, None),
            P(),
            P(),
            P(),
            P(None, None, "wave", "lev"),
            P(),
            P(),
        ),
        out_specs=(P(("wave", "lev"), None, None, None), P(None, None, "wave", "lev")),
        check_vma=False,
    )
```

```python
import functools
import math

import jax
import jax.numpy as jnp
from jax import lax
from jax.experimental import pallas as pl
from jax.experimental.pallas import tpu as pltpu
from jax.sharding import PartitionSpec as P

TRUNC = 1280
NLON = 2560
HALF = NLON // 2
SUBSTEPS = 2
COURANT = 0.6
LANES = 128
FOLD = HALF + LANES
PIECE_ROWS = 64
DEPTH = 4
UNIT = 8
HALO = 2
BF, F32 = jnp.bfloat16, jnp.float32


def table_kernel(cos_ref, sin_ref, turned_cos_ref, turned_sin_ref, a_ref, b_ref, out_ref):
    step = pl.program_id(0)
    owners = cos_ref.shape[0]
    for row in range(a_ref.shape[0]):
        for block in range(FOLD // LANES):
            part = slice(block * LANES, (block + 1) * LANES)
            cos, sin = (turned_cos_ref, turned_sin_ref) if block % 2 else (cos_ref, sin_ref)
            value = cos[...] * a_ref[row, :, part] - sin[...] * b_ref[row, :, part]
            out_ref[row * owners : (row + 1) * owners, part] = value.astype(BF)

    @pl.when(step == 0)
    def _():
        top = out_ref[:16, :].astype(F32)
        first = lax.broadcasted_iota(jnp.int32, top.shape, 0) == 0
        out_ref[:16, :] = jnp.where(first, 0.5 * top, top).astype(BF)


def fourier_table(owners, m_count):
    unit = 2.0 * math.pi / NLON
    owner = jnp.arange(owners, dtype=jnp.int32)[:, None]
    lane = jnp.arange(LANES, dtype=jnp.int32)[None, :]
    coarse = (m_count * owner * lane % NLON).astype(F32) * unit
    cos_c, sin_c = jnp.cos(coarse), jnp.sin(coarse)
    turn = jnp.where(owner % 2 == 1, -1.0, 1.0).astype(F32)
    inner = jnp.arange(m_count, dtype=jnp.int32)[:, None]
    fine = (inner * jnp.arange(FOLD, dtype=jnp.int32)[None, :] % NLON).astype(F32) * unit
    cos, sin = jnp.cos(fine), jnp.sin(fine)
    a = 2.0 * jnp.concatenate([cos, -sin])
    b = 2.0 * jnp.concatenate([sin, cos])
    rows = 2 * m_count
    coarse_spec = pl.BlockSpec((owners, LANES), lambda i: (0, 0))
    fine_spec = pl.BlockSpec((PARTS, 1, FOLD), lambda i: (i, 0, 0))
    out_spec = pl.BlockSpec((PARTS * owners, FOLD), lambda i: (i, 0))
    shape = jax.ShapeDtypeStruct((owners * rows, FOLD), BF)
    return pl.pallas_call(
        table_kernel,
        grid=(rows // PARTS,),
        in_specs=[coarse_spec] * 4 + [fine_spec] * 2,
        out_specs=out_spec,
        out_shape=shape,
        cost_estimate=pl.CostEstimate(flops=6 * TRUNC * FOLD, bytes_accessed=4 * TRUNC * FOLD, transcendentals=0),
        name="fourier_table",
    )(cos_c, sin_c, turn * cos_c, turn * sin_c, a[:, None], b[:, None])


def exchanged(x, turned):
    lanes = lane_ids(x[0].shape)
    low, even = lanes < 64, (lanes & 32) == 0
    pairs = [(jnp.where(low, x[i], turned[i + 2]), jnp.where(low, turned[i], x[i + 2])) for i in range(2)]
    out = []
    for first, second in zip(*pairs):
        out.append(jnp.where(even, first, pltpu.roll(second, 32, 1)))
        out.append(jnp.where(even, pltpu.roll(first, LANES - 32, 1), second))
    return out


def kept(m, shape, part_rows):
    row = lax.broadcasted_iota(jnp.int32, shape, 0)
    k = lax.broadcasted_iota(jnp.int32, shape, 1)
    return (k < TRUNC - m) & ((row < part_rows) | (m > 0)), k % 2 == 0


def table_copy(leg_ref, table_ref, sem, m):
    slot = m % DEPTH
    return pltpu.make_async_copy(leg_ref.at[m], table_ref.at[slot], sem.at[slot])


def start_copies(leg_ref, table_ref, sem, step, count):
    @pl.when(step == 0)
    def _():
        for m in range(DEPTH - 1):
            table_copy(leg_ref, table_ref, sem, m).start()

    @pl.when(step + DEPTH - 1 < count)
    def _():
        table_copy(leg_ref, table_ref, sem, step + DEPTH - 1).start()


def inverse_kernel(geometry, first_ref, spec_ref, leg_ref, out_ref, z_ref, q_ref, x_ref, turned_ref, table_ref, sem):
    waves, levs, groups, bands, band_groups, m_count = geometry
    half_rows = leg_ref.shape[1]
    step = pl.program_id(0)
    start_copies(leg_ref, table_ref, sem, step, m_count)
    spec = spec_ref[0].astype(F32)
    keep, even = kept(first_ref[0] + step, spec.shape, spec.shape[0] // 2)
    spec = jnp.where(keep, spec, 0.0)
    other = jnp.where(even, spec, -spec)
    stacked = jnp.concatenate([spec, other, other, spec], axis=0).astype(BF)
    table_copy(leg_ref, table_ref, sem, step).wait()
    values = lax.dot_general(table_ref[step % DEPTH], stacked, (((1,), (1,)), ((), ())), preferred_element_type=F32)
    x_ref[...] = values[:, :LANES]
    turned_ref[...] = values[:, LANES:]
    quarter = half_rows // 4
    lines = [pl.ds(q, quarter, stride=4) for q in range(4)]
    for part, value in enumerate(exchanged([x_ref[i, :] for i in lines], [turned_ref[i, :] for i in lines])):
        z_ref[pl.ds(step * half_rows + part * quarter, quarter), :] = value

    @pl.when(step == m_count - 1)
    def _():
        q_ref[...] = jnp.zeros_like(q_ref)

        def of_wave(wave, carry):
            south = (wave >= bands).astype(jnp.int32)
            band = jnp.where(wave >= bands, waves - 1 - wave, wave)
            for lev in range(levs):
                for g in range(groups):
                    slot = lev * groups + g
                    at = band * band_groups + jnp.where(south == 1, band_groups + HALO - 1 - slot, slot - HALO)
                    over = at >= bands * band_groups
                    line = jnp.where(over, 2 * bands * band_groups - 1 - at, jnp.maximum(at, 0))
                    base = line + jnp.where(over, 1 - south, south) * (half_rows // 2)
                    for c in range(2):
                        for row, count, skip in moves(geometry, half_rows, slot, c):
                            start = base + (c * (half_rows // 4) + skip)
                            q_ref[lev, row : row + count] = z_ref[pl.ds(start, count, stride=half_rows), :]
                out_ref[wave * levs + lev] = q_ref[lev].astype(BF)
            return carry

        lax.fori_loop(0, waves, of_wave, 0)


def direct_kernel(geometry, first_ref, values_ref, weights_ref, leg_ref, out_ref, z_ref, q_ref, x_ref, w_ref, table_ref, sem):
    waves, levs, groups, bands, band_groups, m_count = geometry
    half_rows = leg_ref.shape[1]
    step = pl.program_id(0)
    start_copies(leg_ref, table_ref, sem, step, m_count)

    @pl.when(step == 0)
    def _():
        for q in range(4):
            rows = pl.ds(q * (half_rows // 4), half_rows // 4)
            w_ref[rows, :] = jnp.broadcast_to(weights_ref[:, q : q + 1], (half_rows // 4, LANES))

        def of_wave(wave, carry):
            south = (wave >= bands).astype(jnp.int32)
            band = jnp.where(wave >= bands, waves - 1 - wave, wave)
            for lev in range(levs):
                q_ref[lev] = values_ref[wave * levs + lev].astype(F32)
                for g in range(groups):
                    slot = lev * groups + g
                    if HALO <= slot < band_groups + HALO:
                        inside = jnp.where(south == 1, band_groups + HALO - 1 - slot, slot - HALO)
                        base = band * band_groups + inside + south * (half_rows // 2)
                        for c in range(2):
                            for row, count, skip in moves(geometry, half_rows, slot, c):
                                start = base + (c * (half_rows // 4) + skip)
                                z_ref[pl.ds(start, count, stride=half_rows), :] = q_ref[lev, row : row + count]
            return carry

        lax.fori_loop(0, waves, of_wave, 0)

    quarter = half_rows // 4
    x = [z_ref[pl.ds(step * half_rows + part * quarter, quarter), :] for part in range(4)]
    x = [x[0] + x[2], x[1] + x[3], x[0] - x[2], x[1] - x[3]]
    for q, value in enumerate(exchanged(x, [pltpu.roll(i, 64, 1) for i in x])):
        x_ref[pl.ds(q, quarter, stride=4), :] = w_ref[pl.ds(q * quarter, quarter), :] * value
    paired = x_ref[...].astype(BF)
    table_copy(leg_ref, table_ref, sem, step).wait()
    folded = lax.dot_general(paired, table_ref[step % DEPTH], (((0,), (0,)), ((), ())), preferred_element_type=F32)
    half = folded.shape[0] // 2
    keep, even = kept(first_ref[0] + step, (half, folded.shape[1]), half // 2)
    chosen = jnp.where(even, folded[:half], folded[half:])
    out_ref[0] = jnp.where(keep, chosen, 0.0).astype(BF)


def moves(geometry, half_rows, slot, c):
    m_count = geometry[-1]
    units = 2 * geometry[2]
    unit = 2 * (slot % geometry[2]) + c
    tail = m_count - UNIT
    return (unit * UNIT, UNIT, 0), (units * UNIT + unit * tail, tail, UNIT * half_rows)


def legendre_call(kernel, name, extra, first, operands, in_specs, out_spec, out_shape, geometry, legendre):
    m_count, half_rows, k_count = legendre.shape
    levs = geometry[1]
    return pl.pallas_call(
        functools.partial(kernel, geometry),
        grid=(m_count,),
        in_specs=[pl.BlockSpec(memory_space=pltpu.SMEM)]
        + in_specs
        + [pl.BlockSpec(memory_space=pl.ANY)],
        out_specs=out_spec,
        out_shape=out_shape,
        scratch_shapes=[
            pltpu.VMEM((m_count * half_rows, LANES), F32),
            pltpu.VMEM((levs, PIECE_ROWS, LANES), F32),
        ]
        + [pltpu.VMEM((half_rows, LANES), F32)] * extra
        + [pltpu.VMEM((DEPTH, half_rows, k_count), BF), pltpu.SemaphoreType.DMA((DEPTH,))],
        cost_estimate=pl.CostEstimate(
            flops=2 * legendre.size * LANES, bytes_accessed=2 * legendre.size + 5 * 10**6, transcendentals=0
        ),
        name=name,
    )(first.reshape(1), *operands, legendre)


PARTS = 5


def grid_kernel(owners, steps, table_ref, *refs):
    value_refs, warm_refs, (heat_ref, out_ref, pack_ref, fold_ref) = refs[:2], refs[2:4], refs[4:]
    step = pl.program_id(0)
    lines = value_refs[0].shape[0]
    groups = lines // LANES
    rows = out_ref.shape[1]
    m_count = steps * PARTS // 2

    @pl.when(step == 0)
    def _():
        scale = 0.5 / math.sqrt(NLON)
        start = lane_ids((lines, LANES)) == 0
        columns = lines // 32
        levels = warm_refs[0].shape[0] // columns
        below = heat_ref.shape[0] // 2

        def tendency(side, block):
            part = slice(block * LANES, (block + 1) * LANES)
            there = slice(side * HALF + block * LANES, side * HALF + (block + 1) * LANES)
            value = value_refs[side][:, part].astype(F32)
            pieces = []
            for at in range(columns):
                cell = at // (columns // groups) * levels
                heat = heat_ref[cell : cell + levels, there] + heat_ref[below + cell : below + cell + levels, there]
                warm = warm_refs[side][at * levels : (at + 1) * levels, part] + heat
                pieces += [value[at * 32 : at * 32 + 2 * levels], warm.astype(BF).astype(F32)]
                pieces += [value[at * 32 + 3 * levels : (at + 1) * 32]]
            return jnp.concatenate(pieces, axis=0)

        for block in range(HALF // LANES):
            west, east = tendency(0, block), tendency(1, block)
            total = west + east
            if block == 0:
                total = jnp.where(start, west, total)
                fold_ref[0, :, HALF:] = jnp.where(start, scale * east, 0.0).astype(BF)
                fold_ref[1, :, HALF:] = jnp.zeros((lines, LANES), BF)
            fold_ref[0, :, block * LANES : (block + 1) * LANES] = (scale * total).astype(BF)
            fold_ref[1, :, block * LANES : (block + 1) * LANES] = (scale * (west - east)).astype(BF)

    part_c = step // (steps // 2)
    result = lax.dot_general(
        table_ref[...], fold_ref[part_c], (((1,), (1,)), ((), ())), preferred_element_type=F32
    )
    first = (lax.broadcasted_iota(jnp.int32, (owners, LANES), 0) == 0) & (step == 0)
    tail = m_count - UNIT
    for part in range(PARTS):
        m = step % (steps // 2) * PARTS + part
        for g in range(groups):
            unit = 2 * g + part_c
            start = jnp.where(m < UNIT, unit * UNIT + m, 2 * groups * UNIT + unit * tail + m - UNIT)
            value = result[part * owners : (part + 1) * owners, g * LANES : (g + 1) * LANES]
            if part == 0:
                value = jnp.where(first, 2.0 * value, value)
            pack_ref[pl.ds(start, owners, stride=rows), :] = value

    @pl.when(step == steps - 1)
    def _():
        blank = jnp.zeros((owners, LANES), F32)
        for row in range(groups * PARTS * steps, rows):
            pack_ref[pl.ds(row, owners, stride=rows), :] = blank
        out_ref[...] = pack_ref[...].reshape(out_ref.shape).astype(BF)


def grid_to_pieces(table, values, warm, heating, owners):
    steps = table.shape[0] // owners // PARTS
    return pl.pallas_call(
        functools.partial(grid_kernel, owners, steps),
        grid=(steps,),
        in_specs=[
            pl.BlockSpec((PARTS * owners, FOLD), lambda i: (i, 0)),
            *[pl.BlockSpec(value.shape, lambda i: (0, 0)) for value in (*values, *warm, heating)],
        ],
        out_specs=pl.BlockSpec((owners, PIECE_ROWS, LANES), lambda i: (0, 0, 0)),
        out_shape=jax.ShapeDtypeStruct((owners, PIECE_ROWS, LANES), BF),
        scratch_shapes=[
            pltpu.VMEM((owners * PIECE_ROWS, LANES), F32),
            pltpu.VMEM((2, values[0].shape[0], FOLD), BF),
        ],
        cost_estimate=pl.CostEstimate(
            flops=2 * table.size * values[0].shape[0], bytes_accessed=2 * table.size + 5 * 10**6, transcendentals=0
        ),
        name="grid_to_pieces",
    )(table, *values, *warm, heating)


def lane_ids(shape):
    return lax.broadcasted_iota(jnp.int32, shape, len(shape) - 1)


def edge_columns_kernel(tr_ref, head_ref, tail_ref, pad):
    levels, rows, count, cols = tr_ref.shape
    lanes = lane_ids((count, LANES))
    gap = LANES - HALO - cols
    for level in range(levels):
        head = jnp.zeros((count, LANES), F32)
        tail = head
        pad[level, :, :, :cols] = tr_ref[level]
        for r in range(rows):
            line = pad[level, r]
            head = jnp.where((lanes >> 1) == r, pltpu.roll(line, 2 * r, 1), head)
            tail = jnp.where(
                (lanes >> 1) == r + gap // 2, pltpu.roll(line, (2 * r + gap - cols + HALO) % LANES, 1), tail
            )
        head_ref[level] = head.astype(BF)
        tail_ref[level] = tail.astype(BF)


def both_sides(west, east, cols, lanes):
    return jnp.where(lanes < LANES - HALO - cols, east.astype(F32), west.astype(F32))


def with_columns(line, r, sides, cols, lanes):
    here = ((lanes >> 1) == cols // 2) | ((lanes >> 1) == LANES // 2 - 1)
    return jnp.where(here, pltpu.roll(sides, (cols - 2 * r) % LANES, 1), line)


def edge_rows_kernel(rows, first_ref, last_ref, west_ref, east_ref, top_ref, low_ref, line):
    levels, _, count, cols = first_ref.shape
    lanes = lane_ids((count, LANES))
    for level in range(levels):
        sides = both_sides(west_ref[level], east_ref[level], cols, lanes)
        for at in range(HALO):
            for src, out, r in ((first_ref, top_ref, at), (last_ref, low_ref, rows - HALO + at)):
                line[:, :cols] = src[level, at]
                out[level, at] = with_columns(line[...], r, sides, cols, lanes).astype(BF)


def chemistry_kernel(
    total_rows, first_ref, tr_ref, north_ref, south_ref, west_ref, east_ref, u_ref, v_ref, react_ref, heat_ref,
    mix_ref, heating_ref, x_ref, y_ref, coef_ref,
):
    rows, tracers, cols = tr_ref.shape[1:]
    deep = rows + 2 * HALO
    lanes = lane_ids((tracers, LANES))
    sides = both_sides(west_ref[0], east_ref[0], cols, lanes)
    for at in range(HALO):
        x_ref[at] = north_ref[0, at].astype(F32)
        x_ref[rows + HALO + at] = south_ref[0, at].astype(F32)
    x_ref[HALO : HALO + rows, :, :cols] = tr_ref[0]
    for r in range(rows):
        x_ref[HALO + r] = with_columns(x_ref[HALO + r], r, sides, cols, lanes)
    u, v = u_ref[0], v_ref[0]
    face_u = 0.5 * (u + pltpu.roll(u, LANES - 1, 1))
    east_up, east_down = COURANT * jnp.maximum(face_u, 0.0), COURANT * jnp.minimum(face_u, 0.0)
    face_v = 0.5 * (v + pltpu.roll(v, deep - 1, 0))
    row = first_ref[0] - HALO + lax.broadcasted_iota(jnp.int32, face_v.shape, 0)
    face_v = jnp.where((row >= 0) & (row + 1 <= total_rows - 1), face_v, 0.0)
    south_up, south_down = COURANT * jnp.maximum(face_v, 0.0), COURANT * jnp.minimum(face_v, 0.0)
    coef_ref[0] = 1.0 - east_up + pltpu.roll(east_down, 1, 1) - south_up + pltpu.roll(south_down, 1, 0)
    coef_ref[1] = -east_down
    coef_ref[2] = pltpu.roll(east_up, 1, 1)
    coef_ref[3] = -south_down
    coef_ref[4] = pltpu.roll(south_up, 1, 0)
    react = react_ref[...]

    def moved(src, r):
        q = src[r]
        return (
            coef_ref[0, r : r + 1] * q
            + coef_ref[1, r : r + 1] * pltpu.roll(q, LANES - 1, 1)
            + coef_ref[2, r : r + 1] * pltpu.roll(q, 1, 1)
            + coef_ref[3, r : r + 1] * src[r + 1]
            + coef_ref[4, r : r + 1] * src[r - 1]
        )

    def step(src, r):
        both = jnp.concatenate([moved(src, r), moved(src, r + 1)], axis=1)
        high = both.astype(BF)
        low = (both - high.astype(F32)).astype(BF)
        return both + jnp.dot(react, jnp.concatenate([high, high, low], axis=0), preferred_element_type=F32)

    for r in range(1, deep - 1, 2):
        both = step(x_ref, r)
        y_ref[r] = both[:, :LANES]
        y_ref[r + 1] = both[:, LANES:]
    heat = jnp.broadcast_to(heat_ref[...], (tracers, LANES))
    heating_ref[0] = jnp.zeros_like(heating_ref[0])
    for r in range(HALO, rows + HALO, 2):
        both = step(y_ref, r)
        for at in range(2):
            one = both[:, at * LANES : (at + 1) * LANES]
            mix_ref[0, r - HALO + at] = one[:, :cols]
            warm = jnp.sum(heat * one, axis=0, keepdims=True)
            heating_ref[0, r + at : r + at + 1] = jnp.where(lanes[:1] < cols, warm, 0.0)


def shift(value, axis, by):
    count = lax.axis_size(axis)
    return lax.ppermute(value, axis, [(i, (i + by) % count) for i in range(count)])


def edge_columns(tracers):
    levels, rows, count, cols = tracers.shape
    pair = levels // 4
    return pl.pallas_call(
        edge_columns_kernel,
        grid=(levels // pair,),
        in_specs=[pl.BlockSpec((pair, rows, count, cols), lambda l: (l, 0, 0, 0))],
        out_specs=[pl.BlockSpec((pair, count, LANES), lambda l: (l, 0, 0))] * 2,
        out_shape=[jax.ShapeDtypeStruct((levels, count, LANES), BF)] * 2,
        scratch_shapes=[pltpu.VMEM((pair, rows, count, LANES), F32)],
        cost_estimate=pl.CostEstimate(flops=10**7, bytes_accessed=7 * 10**6, transcendentals=0),
        name="edge_columns",
    )(tracers)


def edge_rows(tracers, west, east):
    levels, rows, count, cols = tracers.shape
    row_shape = jax.ShapeDtypeStruct((levels, HALO, count, LANES), BF)
    some = levels // 2
    return pl.pallas_call(
        functools.partial(edge_rows_kernel, rows),
        grid=(levels // some,),
        in_specs=[
            pl.BlockSpec((some, HALO, count, cols), lambda l: (l, 0, 0, 0)),
            pl.BlockSpec((some, HALO, count, cols), lambda l: (l, rows // HALO - 1, 0, 0)),
            pl.BlockSpec((some, count, LANES), lambda l: (l, 0, 0)),
            pl.BlockSpec((some, count, LANES), lambda l: (l, 0, 0)),
        ],
        out_specs=[pl.BlockSpec((some, HALO, count, LANES), lambda l: (l, 0, 0, 0))] * 2,
        scratch_shapes=[pltpu.VMEM((count, LANES), F32)],
        out_shape=[row_shape] * 2,
        cost_estimate=pl.CostEstimate(flops=10**6, bytes_accessed=2 * 10**6, transcendentals=0),
        name="edge_rows",
    )(tracers, tracers, west, east)


def chemistry(tracers, halos, winds, reaction, heat_coeff, row_first, total_rows):
    levels, rows, count, cols = tracers.shape
    deep = rows + 2 * HALO
    high = reaction.astype(BF)
    low = (reaction - high.astype(F32)).astype(BF)
    react = jnp.concatenate([high, low, high], axis=1)
    heat = heat_coeff[:, None]
    tr_spec = pl.BlockSpec((1, rows, count, cols), lambda l: (l, 0, 0, 0))
    col_spec = pl.BlockSpec((1, count, LANES), lambda l: (l, 0, 0))
    row_spec = pl.BlockSpec((1, HALO, count, LANES), lambda l: (l, 0, 0, 0))
    whole = lambda shape: pl.BlockSpec(shape, lambda l: (0,) * len(shape))
    return pl.pallas_call(
        functools.partial(chemistry_kernel, total_rows),
        grid=(levels,),
        in_specs=[
            pl.BlockSpec(memory_space=pltpu.SMEM),
            tr_spec,
            row_spec,
            row_spec,
            col_spec,
            col_spec,
            pl.BlockSpec((1, deep, LANES), lambda l: (l, 0, 0)),
            pl.BlockSpec((1, deep, LANES), lambda l: (l + levels, 0, 0)),
            whole(react.shape),
            whole(heat.shape),
        ],
        out_specs=[tr_spec, pl.BlockSpec((1, deep, LANES), lambda l: (l, 0, 0))],
        out_shape=[
            jax.ShapeDtypeStruct(tracers.shape, F32),
            jax.ShapeDtypeStruct((levels, deep, LANES), F32),
        ],
        scratch_shapes=[
            pltpu.VMEM((deep, count, LANES), F32),
            pltpu.VMEM((deep, count, LANES), F32),
            pltpu.VMEM((5, deep, LANES), F32),
        ],
        cost_estimate=pl.CostEstimate(flops=10**9, bytes_accessed=16 * 10**6, transcendentals=0),
        name="chemistry",
    )(row_first.reshape(1), tracers, *halos, winds, winds, react, heat)


def body(spectra, legendre, gauss_weights, phys_matrix, phys_bias, tracers, reaction, heat_coeff):
    waves = lax.axis_size("wave")
    levs = lax.axis_size("lev")
    both = ("wave", "lev")
    wave, lev = lax.axis_index("wave"), lax.axis_index("lev")
    m_count, k_count, _, fields = spectra.shape
    half_rows = legendre.shape[1]
    levels, _, chem_rows, chem_cols = tracers.shape
    ratio = NLON // (chem_cols * levs)
    bands = waves // 2
    groups = (chem_rows + 2 * HALO) // levs
    width = 2 * fields

    owners = waves * levs
    geometry = (waves, levs, groups, bands, chem_rows, m_count)
    first_m = (wave * levs + lev) * m_count
    piece_shape = (owners, PIECE_ROWS, LANES)
    piece_spec = pl.BlockSpec(piece_shape, lambda m: (0, 0, 0))
    spec_spec = pl.BlockSpec((1, width, k_count), lambda m: (m, 0, 0))
    used = groups * 2 * m_count
    tracers = tracers.transpose(0, 2, 1, 3)

    pieces = legendre_call(
        inverse_kernel,
        "to_latitude",
        2,
        first_m,
        [spectra.transpose(0, 2, 3, 1).reshape(m_count, width, k_count)],
        [spec_spec],
        piece_spec,
        jax.ShapeDtypeStruct(piece_shape, BF),
        geometry,
        legendre,
    )
    spread = lax.all_to_all(pieces, both, split_axis=0, concat_axis=0, tiled=True)
    head, tail = edge_columns(tracers)
    west, east = shift(tail, "lev", 1), shift(head, "lev", -1)
    table = fourier_table(owners, m_count)
    spread = spread[:, :used].transpose(1, 0, 2)
    tiles = groups * 2 * UNIT
    spread = jnp.concatenate(
        [spread[:tiles].reshape(groups, 2, UNIT, owners, LANES), spread[tiles:].reshape(groups, 2, -1, owners, LANES)],
        axis=2,
    ).reshape(groups, 2, TRUNC, LANES)

    sums = jnp.einsum("gckn,ckj->cgnj", spread, table.reshape(2, TRUNC, FOLD), preferred_element_type=F32)
    cosine, sine, turn = sums[0, ..., :HALF], sums[1, ..., :HALF], sums[0, ..., HALF : HALF + 1]
    turned = jnp.where(jnp.arange(HALF, dtype=jnp.int32) == 0, turn, cosine - sine)
    halves = [value.astype(BF).reshape(groups, ratio, fields, HALF) for value in (cosine + sine, turned)]

    lane = jnp.arange(LANES, dtype=jnp.int32)
    column = jnp.where(lane < LANES - HALO, lane, lane - LANES)
    column = (column[None, :] + chem_cols * jnp.arange(levs, dtype=jnp.int32)[:, None]) % (chem_cols * levs)
    held = (lane < chem_cols + HALO) | (lane >= LANES - HALO)
    column = jnp.where(held[None, :], column, -1).reshape(levs * LANES)
    order = jnp.arange(HALF, dtype=jnp.int32)
    cells = [order // ratio, jnp.where(order == 0, HALF, NLON - order) // ratio]
    means = [jnp.where(cell[:, None] == column[None, :], 1.0 / ratio**2, 0.0).astype(BF) for cell in cells]
    cell = jnp.concatenate(cells)
    winds = sum(
        jnp.einsum("gqfj,jx->gqfx", half[:, :, : 2 * levels], part, preferred_element_type=F32).sum(axis=1)
        for half, part in zip(halves, means)
    )
    winds = winds.reshape(groups * 2 * levels, levs, LANES).transpose(1, 0, 2)
    winds, west, east = lax.optimization_barrier((winds, west, east))
    top, low = edge_rows(tracers, west, east)
    halos = (shift(low, "wave", 1), shift(top, "wave", -1), west, east)
    winds = lax.all_to_all(winds, "lev", split_axis=0, concat_axis=0, tiled=True)
    winds = winds.reshape(levs * groups, 2 * levels, LANES).transpose(1, 0, 2)

    mixing, heating = chemistry(
        tracers, halos, winds, reaction, heat_coeff, wave * chem_rows, chem_rows * waves
    )
    heating = heating.transpose(1, 0, 2).reshape(levs, groups * levels, LANES)
    heating = lax.all_to_all(heating, "lev", split_axis=0, concat_axis=0, tiled=True)
    heating = heating.transpose(1, 0, 2).reshape(groups * levels, levs * LANES)
    high = heating.astype(BF)
    low = (heating - high.astype(F32)).astype(BF)
    column = jnp.where(lane[None, :] < chem_cols, lane + chem_cols * jnp.arange(levs, dtype=jnp.int32)[:, None], -1)
    copied = (column.reshape(levs * LANES)[:, None] == cell[None, :]).astype(BF)
    heating = jnp.dot(jnp.concatenate([high, low]), copied, preferred_element_type=F32)

    values, warm = [], []
    for half in halves:
        physics = jnp.tanh(
            jnp.einsum("ef,gqfj->gqej", phys_matrix, half.astype(F32), precision=lax.Precision.HIGHEST)
            + phys_bias[:, None]
        )
        values.append(physics.astype(BF).reshape(groups * ratio * fields, HALF))
        warm.append(physics[:, :, 2 * levels : 3 * levels].reshape(groups * ratio * levels, HALF))

    coeffs = grid_to_pieces(table, values, warm, heating, owners)
    values = lax.all_to_all(coeffs, both, split_axis=0, concat_axis=0, tiled=True)

    result = legendre_call(
        direct_kernel,
        "to_spectral",
        2,
        first_m,
        [values, gauss_weights.reshape(half_rows // 4, 4)],
        [piece_spec, pl.BlockSpec((half_rows // 4, 4), lambda m: (0, 0))],
        spec_spec,
        jax.ShapeDtypeStruct((m_count, width, k_count), BF),
        geometry,
        legendre,
    )
    result = result.reshape(m_count, 2, fields, k_count).transpose(0, 3, 1, 2)
    mixing = mixing.transpose(0, 2, 1, 3)
    return (result, mixing)


def solution(mesh):
    return jax.shard_map(
        body,
        mesh=mesh,
        in_specs=(
            P(("wave", "lev"), None, None, None),
            P(("wave", "lev"), None, None),
            P(),
            P(),
            P(),
            P(None, None, "wave", "lev"),
            P(),
            P(),
        ),
        out_specs=(P(("wave", "lev"), None, None, None), P(None, None, "wave", "lev")),
        check_vma=False,
    )
```
